32 devices in a mesh: wide: 8 (over z, x), narrow: 4 (over y, core).
Axes of the slice: x: 2, y: 2, z: 4, core: 2. Of those that a mesh axis runs over, the one named last changes fastest.
Arguments:
- displacement: float32 [3, 3, 128, 128, 384], P(None, None, 'wide', 'narrow'), may hold values from -6 to 6
- material: int32 [128, 128, 24], P('wide', 'narrow'), may hold values 0 or 1
- level_set: float32 [384, 128, 128], P('wide', 'narrow'), may hold values from -6 to 6
Outputs:
- level_next: float32 [384, 128, 128], P('wide', 'narrow')
- speed: float32 [384, 128, 128], P('wide', 'narrow')
The draws below stay inside these ranges and needn't reach their ends.
All inputs are finite; a program needn't handle non-finite values. No bound on the sum of `material` on one device may be relied on, other than what follows from the above.
Results may differ from the reference program's by a relative error of at most 0.00002.
Values sent between devices are 32-bit elements; how exact they have to be, the bound alone decides.
A program may use at most 192 MiB of HBM per device.

```python
import jax
import jax.numpy as jnp
from jax import lax

BZ = 16
EXT_PASSES = 4
HJ_STEPS = 3
NX = 128
NY = 128
NZ = 384


def set_ends(array, stream_key, smallest, high):
    extent = array.shape
    place = [jax.random.randint(jax.random.fold_in(stream_key, axis), (), 0, extent[axis]) for axis in range(len(extent))]
    array = array.at[tuple(place)].set(smallest)
    longest = extent.index(max(extent))
    place[longest] = (place[longest] + 1) % extent[longest]
    return array.at[tuple(place)].set(high)


def block_scale(rng, dims, cuts, least, high):
    loudness = 1.0
    for axis_at, blocks in cuts:
        heights = jax.random.uniform(jax.random.fold_in(jax.random.fold_in(rng, 6), axis_at), (blocks,), jnp.float32, least / len(cuts), high / len(cuts))
        loudness = loudness * jnp.repeat(jnp.exp(heights), dims[axis_at] // blocks).reshape((-1,) + (1,) * (len(dims) - 1 - axis_at))
    return loudness


def gaussian(stream_key, shape, scale, bound, cuts=(), held_as=jnp.bfloat16):
    array = jax.random.normal(stream_key, shape, jnp.float32) * scale
    if len(cuts) > 0:
        array = block_scale(stream_key, shape, cuts, -0.22, 0.18) * array
    return jnp.clip(array, min=-bound, max=bound).astype(held_as)


def setup_inputs(seed: int = 0) -> dict:
    streams_of = jax.random.split(jax.random.key(seed), 4)
    return {
        "displacement": gaussian(streams_of[0], (3, 3, NX, NY, NZ), 1.0, 6.0, ((2, 8), (3, 4)), jnp.float32),
        "material": set_ends((jax.random.randint(streams_of[1], (NX, NY, NZ // BZ), 0, 4) < 3).astype(jnp.int32), jax.random.fold_in(streams_of[1], 1), 0, 1),
        "level_set": gaussian(streams_of[2], (NZ, NY, NX), 1.0, 6.0, ((0, 8), (1, 4)), jnp.float32),
    }


SHEAR = 0.384615
LAME = 0.576923
WENO_EPS = 1e-06
TIME_STEP = 0.3
VAL_TAPS = (1.0 / 48.0, 23.0 / 48.0, 23.0 / 48.0, 1.0 / 48.0)
DER_TAPS = (-1.0 / 8.0, -5.0 / 8.0, 5.0 / 8.0, 1.0 / 8.0)

def apply_taps(padded, taps, axis, count):
    total = taps[0] * lax.slice_in_dim(padded, 1, 1 + count, axis=axis)
    for k in range(1, 4):
        total = total + taps[k] * lax.slice_in_dim(padded, 1 + k, 1 + k + count, axis=axis)
    return total

def strain_energy(grad_x, grad_y, grad_z, stiffness):
    exx = grad_x[:, 0]
    eyy = grad_y[:, 1]
    ezz = grad_z[:, 2]
    exy = 0.5 * (grad_y[:, 0] + grad_x[:, 1])
    exz = 0.5 * (grad_z[:, 0] + grad_x[:, 2])
    eyz = 0.5 * (grad_z[:, 1] + grad_y[:, 2])
    trace = exx + eyy + ezz
    square = exx * exx + eyy * eyy + ezz * ezz + 2.0 * (exy * exy + exz * exz + eyz * eyz)
    density = SHEAR * square + 0.5 * LAME * trace * trace
    return stiffness * lax.optimization_barrier(jnp.sum(density, axis=0))

def neighbour_mean(padded):
    wider = jnp.pad(padded, ((0, 0), (0, 0), (1, 1)))
    total = wider[2:, 1:-1, 1:-1] + wider[:-2, 1:-1, 1:-1]
    total = total + wider[1:-1, 2:, 1:-1] + wider[1:-1, :-2, 1:-1]
    total = total + wider[1:-1, 1:-1, 2:] + wider[1:-1, 1:-1, :-2]
    return total * (1.0 / 6.0)

def weno_side(v1, v2, v3, v4, v5):
    p_one = v1 / 3.0 - 7.0 * v2 / 6.0 + 11.0 * v3 / 6.0
    p_two = -v2 / 6.0 + 5.0 * v3 / 6.0 + v4 / 3.0
    p_three = v3 / 3.0 + 5.0 * v4 / 6.0 - v5 / 6.0
    b_one = 13.0 / 12.0 * (v1 - 2.0 * v2 + v3) ** 2 + 0.25 * (v1 - 4.0 * v2 + 3.0 * v3) ** 2
    b_two = 13.0 / 12.0 * (v2 - 2.0 * v3 + v4) ** 2 + 0.25 * (v2 - v4) ** 2
    b_three = 13.0 / 12.0 * (v3 - 2.0 * v4 + v5) ** 2 + 0.25 * (3.0 * v3 - 4.0 * v4 + v5) ** 2
    a_one = 0.1 / (WENO_EPS + b_one) ** 2
    a_two = 0.6 / (WENO_EPS + b_two) ** 2
    a_three = 0.3 / (WENO_EPS + b_three) ** 2
    return (a_one * p_one + a_two * p_two + a_three * p_three) / (a_one + a_two + a_three)

def march_step(padded, speed):
    wider = jnp.pad(padded, ((0, 0), (0, 0), (3, 3)), constant_values=1.0)
    size_z = padded.shape[0] - 6
    size_y = padded.shape[1] - 6
    size_x = padded.shape[2]
    centre = wider[3:3 + size_z, 3:3 + size_y, 3:3 + size_x]
    lines = (wider[:, 3:3 + size_y, 3:3 + size_x], wider[3:3 + size_z, :, 3:3 + size_x], wider[3:3 + size_z, 3:3 + size_y, :])
    grow_plus = None
    grow_minus = None
    for axis in range(3):
        line = lines[axis]
        count = centre.shape[axis]
        diffs = lax.slice_in_dim(line, 1, count + 6, axis=axis) - lax.slice_in_dim(line, 0, count + 5, axis=axis)
        parts = [lax.slice_in_dim(diffs, k, k + count, axis=axis) for k in range(6)]
        minus = weno_side(parts[0], parts[1], parts[2], parts[3], parts[4])
        plus = weno_side(parts[5], parts[4], parts[3], parts[2], parts[1])
        term_p = jnp.maximum(jnp.maximum(minus, 0.0) ** 2, jnp.minimum(plus, 0.0) ** 2)
        term_m = jnp.maximum(jnp.minimum(minus, 0.0) ** 2, jnp.maximum(plus, 0.0) ** 2)
        grow_plus = term_p if grow_plus is None else grow_plus + term_p
        grow_minus = term_m if grow_minus is None else grow_minus + term_m
    return centre - TIME_STEP * (jnp.maximum(speed, 0.0) * jnp.sqrt(grow_plus) + jnp.minimum(speed, 0.0) * jnp.sqrt(grow_minus))

def reference(displacement, material, level_set):
    padded = jnp.pad(displacement, ((0, 0), (0, 0), (2, 2), (2, 2), (2, 2)))
    size_x = displacement.shape[2]
    size_y = displacement.shape[3]
    size_z = displacement.shape[4]
    val_z = apply_taps(padded, VAL_TAPS, 4, size_z)
    der_z = apply_taps(padded, DER_TAPS, 4, size_z)
    vv = apply_taps(val_z, VAL_TAPS, 3, size_y)
    vd = apply_taps(val_z, DER_TAPS, 3, size_y)
    dv = apply_taps(der_z, VAL_TAPS, 3, size_y)
    grad_x = apply_taps(vv, DER_TAPS, 2, size_x)
    grad_y = apply_taps(vd, VAL_TAPS, 2, size_x)
    grad_z = apply_taps(dv, VAL_TAPS, 2, size_x)
    stiffness = 0.2 + 0.8 * jnp.repeat(material.astype(jnp.float32), BZ, axis=2)
    energy = strain_energy(grad_x, grad_y, grad_z, stiffness)
    peak = jnp.max(energy)
    velocity = jnp.transpose(energy / (peak + 1e-06) - 0.5, (2, 1, 0))
    weight = 1.0 / (1.0 + 4.0 * level_set * level_set)
    speed = velocity
    for step in range(EXT_PASSES):
        speed = weight * velocity + (1.0 - weight) * neighbour_mean(jnp.pad(speed, ((1, 1), (1, 1), (0, 0))))
    phi = level_set
    for step in range(HJ_STEPS):
        phi = march_step(jnp.pad(phi, ((3, 3), (3, 3), (0, 0)), constant_values=1.0), speed)
    return (phi, speed)
```

```python
import functools

import jax
import jax.numpy as jnp
from jax import lax
from jax.experimental import pallas as pl
from jax.experimental.pallas import tpu as pltpu
from jax.sharding import PartitionSpec as P

BZ = 16
EXT_PASSES = 4
HJ_STEPS = 3
SHEAR = 0.384615
LAME = 0.576923
WENO_EPS = 1e-06
TIME_STEP = 0.3
TAP_SCALE = 1.0 / (48.0 * 48.0 * 8.0)
MARGIN = 3 * (HJ_STEPS - 1) + EXT_PASSES
SIDE = 16
MESH = pl.DeviceIdType.MESH
f32 = jnp.float32


def val_taps(a, b, c, d):
    return (a + d) + 23.0 * (b + c)


def der_taps(a, b, c, d):
    return (d - a) + 5.0 * (c - b)


def z_filters(u):
    size = u.shape[-1]
    rows = u.shape[0]
    lane = lax.broadcasted_iota(jnp.int32, (rows, 128), 1)
    count = size // 128
    tiles = [u[:, t * 128:(t + 1) * 128] for t in range(count)]
    zero = jnp.zeros((rows, 128), f32)
    up = [pltpu.roll(t, 1, 1) for t in tiles]
    one = [pltpu.roll(t, 127, 1) for t in tiles] + [zero]
    two = [pltpu.roll(t, 126, 1) for t in tiles] + [zero]
    vals, ders = [], []
    for t in range(count):
        before = jnp.where(lane == 0, up[t - 1] if t else zero, up[t])
        after = jnp.where(lane == 127, one[t + 1], one[t])
        second = jnp.where(lane >= 126, two[t + 1], two[t])
        vals.append(val_taps(before, tiles[t], after, second))
        ders.append(der_taps(before, tiles[t], after, second))
    return vals, ders


def minus_side(e0, e1, t0, t1, c1, c3, p, q6, r3):
    low = p * (e0 + (c1 + c1)) + q6 * (e0 + t1) + r3 * (t1 + c3)
    return low, (p + q6) + r3


def plus_side(e0, e1, t0, t1, c1, c3, r, q6, p3):
    high = r * (e1 + (c3 + c3)) + q6 * (e1 + t0) + p3 * (t0 + c1)
    return high, (r + q6) + p3


EPS = 0.75 * WENO_EPS


def both_sides(d6, e0, e1, s0, s2, q0, q1, q2, g0, g1, t0, t1):
    c1 = e0 + s0
    c3 = e1 - s2
    a = q0 + g0 * c1
    b = q1 + g0 * e1
    c = q2 + g1 * c3
    a, b, c = a * a, b * b, c * c
    p, q6, r = b * c, 6.0 * (a * c), a * b
    low, low_sum = minus_side(e0, e1, t0, t1, c1, c3, p, q6, 3.0 * r)
    high, high_sum = plus_side(e0, e1, t0, t1, c1, c3, r, q6, 3.0 * p)
    return d6 + low / low_sum, high / high_sum - d6


def godunov(minus, plus):
    up = jnp.maximum(jnp.maximum(minus, plus), 0.0)
    down = jnp.minimum(jnp.minimum(minus, plus), 0.0)
    return up * up, down * down


def along_lanes(mid):
    size = mid.shape[-1]
    lane = lax.broadcasted_iota(jnp.int32, mid.shape, 1)
    first, last = lane == 0, lane == size - 1

    def before(x, edge):
        return jnp.where(first, edge, pltpu.roll(x, 1, 1))

    def after(x, edge):
        return jnp.where(last, edge, pltpu.roll(x, size - 1, 1))

    d_low = mid - before(mid, 0.0)
    d_here = after(mid, 0.0) - mid
    e2 = d_here - d_low
    e1 = before(e2, mid)
    e0 = before(e1, 0.0)
    e3 = after(e2, mid)
    e4 = after(e3, 0.0)
    s = [e1 - e0, e2 - e1, e3 - e2, e4 - e3]
    q = [x * x + EPS for x in s]
    g = [0.75 * x for x in (e1, e2, e3)]
    t = [x + x for x in (e1, e2, e3)]
    c1, c3 = e1 + s[0], e2 - s[2]
    a, b, c = q[0] + g[0] * c1, q[1] + g[0] * e2, q[2] + g[1] * c3
    a, b, c = a * a, b * b, c * c
    low, low_sum = minus_side(e1, e2, t[0], t[1], c1, c3, b * c, 6.0 * (a * c), 3.0 * (a * b))
    c1, c3 = e2 + s[1], e3 - s[3]
    a, b, c = q[1] + g[1] * c1, q[2] + g[1] * e3, q[3] + g[2] * c3
    a, b, c = a * a, b * b, c * c
    high, high_sum = plus_side(e2, e3, t[1], t[2], c1, c3, a * b, 6.0 * (a * c), 3.0 * (b * c))
    return 6.0 * d_low + low / low_sum, high / high_sum - 6.0 * d_here


def along_rows(ref, z, start, count):
    u = [ref[z, pl.ds(start + k, count), :] for k in range(-2, 4)]
    d = [u[k + 1] - u[k] for k in range(5)]
    e = [d[k + 1] - d[k] for k in range(4)]
    s = [e[k + 1] - e[k] for k in range(3)]
    q = [x * x + EPS for x in s]
    return both_sides(
        6.0 * d[2], e[1], e[2], s[0], s[2], q[0], q[1], q[2], 0.75 * e[1], 0.75 * e[2], e[1] + e[1], e[2] + e[2]
    )


def along_planes(ref, gp, gm, z_lo, z_hi, at):
    u = [ref[z_lo - 3 + k, at, :] for k in range(5)]
    d = [u[k + 1] - u[k] for k in range(4)]
    e = [d[k + 1] - d[k] for k in range(3)]
    s = [e[k + 1] - e[k] for k in range(2)]
    q = [x * x + EPS for x in s]
    g = 0.75 * e[1]
    t = e[1] + e[1]
    newest, d_mid, d_new = u[4], d[2], d[3]
    behind = None
    for z in range(z_lo - 1, z_hi):
        plane = ref[z + 3, at, :]
        d_next = plane - newest
        e_next = d_next - d_new
        s_next = e_next - e[2]
        q_next = s_next * s_next + EPS
        g_next = 0.75 * e[2]
        t_next = e[2] + e[2]
        minus, plus = both_sides(
            6.0 * d_mid, e[1], e[2], s[0], s_next, q[0], q[1], q_next, g, g_next, t, t_next
        )
        if behind is not None:
            up, down = godunov(behind, plus)
            gp[z, at, :] = up
            gm[z, at, :] = down
        behind = minus
        newest, d_mid, d_new = plane, d_new, d_next
        e = [e[1], e[2], e_next]
        s = [s[1], s_next]
        q = [q[1], q_next]
        g, t = g_next, t_next


def block_flip(x):
    row = lax.broadcasted_iota(jnp.int32, (8, 128), 0)
    block = lax.broadcasted_iota(jnp.int32, (8, 128), 1) // 16
    far = pltpu.roll(pltpu.roll(x, 4, 0), 64, 1)
    x = jnp.where((row // 4) % 2 == (block // 4) % 2, x, far)
    for bit in (2, 1):
        row_bit, block_bit = (row // bit) % 2, (block // bit) % 2
        down = pltpu.roll(pltpu.roll(x, bit, 0), 128 - 16 * bit, 1)
        up = pltpu.roll(pltpu.roll(x, 8 - bit, 0), 16 * bit, 1)
        x = jnp.where(row_bit == block_bit, x, jnp.where(row_bit > block_bit, down, up))
    return x


def kernel(
    disp, mat, lev, next_ref, speed_ref,
    field, energy, stiff, packed, arrived, phi, peak_out, peak_in, peak_mid, peak_all,
    own_sem, x_send, x_recv, y_send, y_recv, c_send, c_recv, lev_sem, lev_send, lev_recv,
    a_sem, a_send, a_recv, f_send, f_recv, p_send, p_recv, n_send, n_recv,
    *, wide, narrow,
):
    i = lax.axis_index("wide")
    j = lax.axis_index("narrow")
    fields, size_x, size_y, size_z = disp.shape
    own_z, own_y, lanes = lev.shape
    deep, rows, _ = phi.shape
    tiles = size_z // 128
    groups = own_y // 8
    tail = size_y
    has = {(-1, 0): i > 0, (1, 0): i < wide - 1, (0, -1): j > 0, (0, 1): j < narrow - 1}
    for a in (-1, 1):
        for b in (-1, 1):
            has[(a, b)] = has[(a, 0)] & has[(0, b)]
    around = [(-1, 0), (1, 0), (0, -1), (0, 1), (-1, -1), (-1, 1), (1, -1), (1, 1)]

    def remote(src, dst, send, recv, w, n):
        return pltpu.make_async_remote_copy(
            src_ref=src, dst_ref=dst, send_sem=send, recv_sem=recv,
            device_id={"wide": w, "narrow": n}, device_id_type=MESH,
        )

    own_copies = [
        pltpu.make_async_copy(
            disp.at[3 * l:3 * l + 3], field.at[3 * l:3 * l + 3, 0:size_x, 0:size_y], own_sem.at[l]
        )
        for l in range(3)
    ]
    lev_copy = pltpu.make_async_copy(
        lev, phi.at[MARGIN:MARGIN + own_z, SIDE:SIDE + own_y], lev_sem
    )

    def plane_part(dx):
        if dx < 0:
            return slice(0, 2), slice(size_x, size_x + 2)
        if dx > 0:
            return slice(size_x - 1, size_x), slice(size_x + 2, size_x + 3)
        return slice(0, size_x), slice(0, size_x)

    def row_part(dy):
        if dy < 0:
            return slice(0, 2), slice(tail, tail + 2)
        return slice(size_y - 1, size_y), slice(tail + 7, tail + 8)

    def x_copy(dx, l, b):
        src, dst = plane_part(dx)
        at = slice(8 * b, 8 * b + 8)
        k = (dx + 1) // 2
        return remote(
            disp.at[3 * l:3 * l + 3, src, at], field.at[3 * l:3 * l + 3, dst, at],
            x_send.at[k, l, b], x_recv.at[k, l, b], i + dx, j,
        )

    def y_copy(dy, l):
        src, dst = row_part(dy)
        k = (dy + 1) // 2
        return remote(
            disp.at[3 * l:3 * l + 3, :, src], field.at[3 * l:3 * l + 3, 0:size_x, dst],
            y_send.at[k, l], y_recv.at[k, l], i, j + dy,
        )

    def c_copy(dx, dy):
        xs, xd = plane_part(dx)
        ys, yd = row_part(dy)
        k = (dx + 1) + (dy + 1) // 2
        return remote(
            disp.at[:, xs, ys], field.at[:, xd, yd], c_send.at[k], c_recv.at[k], i + dx, j + dy
        )

    def lev_part(step, size, width, before):
        if step < 0:
            return slice(0, width), slice(before + size, before + size + width)
        if step > 0:
            return slice(size - width, size), slice(before - width, before)
        return slice(0, size), slice(before, before + size)

    def lev_send_copy(k):
        dx, dy = around[k]
        zs, zd = lev_part(dx, own_z, MARGIN, MARGIN)
        ys, yd = lev_part(dy, own_y, MARGIN if lanes == 128 else SIDE, SIDE)
        return remote(lev.at[zs, ys], phi.at[zd, yd], lev_send.at[k], lev_recv.at[k], i + dx, j + dy)

    for copy in own_copies:
        copy.start()
    lev_copy.start()

    barrier = pltpu.get_barrier_semaphore()

    @pl.loop(1, wide)
    def _(k):
        pl.semaphore_signal(
            barrier, inc=1, device_id={"wide": (i + k) % wide, "narrow": j}, device_id_type=MESH
        )

    @pl.loop(1, narrow)
    def _(k):
        pl.semaphore_signal(
            barrier, inc=1, device_id={"wide": i, "narrow": (j + k) % narrow}, device_id_type=MESH
        )

    for dx, dy in around[4:]:
        @pl.when(has[(dx, dy)])
        def _(dx=dx, dy=dy):
            pl.semaphore_signal(
                barrier, inc=1, device_id={"wide": i + dx, "narrow": j + dy}, device_id_type=MESH
            )
    beside_x = jnp.where(i > 0, 1, 0) + jnp.where(i < wide - 1, 1, 0)
    beside_y = jnp.where(j > 0, 1, 0) + jnp.where(j < narrow - 1, 1, 0)
    pl.semaphore_wait(barrier, wide - 1 + narrow - 1 + beside_x * beside_y)

    for dy in (-1, 1):
        @pl.when(has[(0, dy)])
        def _(dy=dy):
            for l in range(3):
                y_copy(dy, l).start()
    for b in range(groups):
        for dx in (-1, 1):
            @pl.when(has[(dx, 0)])
            def _(dx=dx, b=b):
                for l in range(3):
                    x_copy(dx, l, b).start()
        if b == 0:
            for dx, dy in around[4:]:
                @pl.when(has[(dx, dy)])
                def _(dx=dx, dy=dy):
                    c_copy(dx, dy).start()
            for k in range(8):
                @pl.when(has[around[k]])
                def _(k=k):
                    lev_send_copy(k).start()

    for dx, planes in ((1, (size_x, size_x + 1)), (-1, (size_x + 2,))):
        @pl.when(jnp.logical_not(has[(dx, 0)]))
        def _(planes=planes):
            @pl.loop(0, fields)
            def _(f):
                for p in planes:
                    field[f, p] = jnp.zeros(field.shape[2:], f32)

    for dy, lo, hi in ((1, tail, tail + 2), (-1, tail + 7, tail + 8)):
        @pl.when(jnp.logical_not(has[(0, dy)]))
        def _(lo=lo, hi=hi):
            @pl.loop(0, fields)
            def _(f):
                for p in range(size_x + 3):
                    field[f, p, lo:hi, :] = jnp.zeros((hi - lo, size_z), f32)

    block = lax.broadcasted_iota(jnp.int32, (mat.shape[1], size_z), 0)
    column = lax.broadcasted_iota(jnp.int32, (mat.shape[1], size_z), 1) // BZ
    spread = jnp.where(block == column, 1.0, 0.0)
    solid = jnp.dot(mat[...].astype(f32), spread, preferred_element_type=f32)
    for t in range(tiles):
        stiff[t] = 0.2 + 0.8 * solid[:, t * 128:(t + 1) * 128]
        energy[t] = jnp.zeros(energy.shape[1:], f32)
    for b in range(groups):
        packed[b] = jnp.zeros(packed.shape[1:], f32)
    peak_out[...] = jnp.zeros(peak_out.shape, f32)

    def inside(z, lo, shape):
        here = i * own_z - MARGIN + z
        row = lax.broadcasted_iota(jnp.int32, shape, 0) + (lo + j * own_y - SIDE)
        end = narrow * own_y
        lowest = jnp.where((here >= 0) & (here < wide * own_z), 0, end)
        return (row >= lowest) & (row < end)

    def energy_phase(val, der, gp, gm):
        def filter_rows(f, p, at, spots):
            vals, ders = z_filters(field[f, p, at, :])
            for t in range(tiles):
                for spot in spots:
                    val[f, p, t, spot, :] = vals[t]
                    der[f, p, t, spot, :] = ders[t]

        tail_spots = (slice(0, 8), slice(8 + size_y, 16 + size_y))

        for l in range(3):
            own_copies[l].wait()

            @pl.loop(0, 3 * size_x)
            def _(k, l=l):
                filter_rows(
                    3 * l + k // size_x, k % size_x, slice(0, size_y), (slice(8, 8 + size_y),)
                )

        for dy in (-1, 1):
            @pl.when(has[(0, -dy)])
            def _(dy=dy):
                for l in range(3):
                    y_copy(dy, l).wait_recv()

        @pl.loop(0, fields)
        def _(f):
            for p in range(size_x):
                filter_rows(f, p, slice(tail, tail + 8), tail_spots)

        def march_planes(f, t, y, planes, out):
            held = []
            for n, p in enumerate(planes):
                v = [[val[f + c, p, t, pl.ds(y + 7 + k, 8), :] for k in range(4)] for c in range(3)]
                w = [[der[f + c, p, t, pl.ds(y + 7 + k, 8), :] for k in range(4)] for c in range(3)]
                vv = [val_taps(*x) for x in v]
                vd = [der_taps(*x) for x in v]
                dv = [val_taps(*x) for x in w]
                held.append((vv[0], vd[0], dv[0], vv[1], vd[1], vv[2], dv[2], dv[1] + vd[2]))
                if len(held) < 4:
                    continue
                line = list(zip(*held))
                held = held[1:]
                exx = der_taps(*line[0])
                eyy = val_taps(*line[4])
                ezz = val_taps(*line[6])
                exy = val_taps(*line[1]) + der_taps(*line[3])
                exz = val_taps(*line[2]) + der_taps(*line[5])
                eyz = val_taps(*line[7])
                trace = exx + eyy + ezz
                square = (exx * exx + eyy * eyy + ezz * ezz) + 0.5 * (exy * exy + exz * exz + eyz * eyz)
                density = (SHEAR * TAP_SCALE * TAP_SCALE) * square
                density = density + (0.5 * LAME * TAP_SCALE * TAP_SCALE) * (trace * trace)
                at = pl.ds(out[n - 3] * size_y + y, 8)
                energy[t, at, :] = energy[t, at, :] + density

        @pl.loop(0, 3 * tiles * groups)
        def _(k):
            y = pl.multiple_of((k % groups) * 8, 8)
            march_planes(
                3 * (k // (tiles * groups)), (k // groups) % tiles, y,
                list(range(size_x)), list(range(1, size_x - 2)),
            )

        lev_copy.wait()
        for k in range(8):
            dx, dy = around[k]

            @pl.when(has[(-dx, -dy)])
            def _(k=k):
                lev_send_copy(k).wait_recv()

        @pl.loop(0, deep)
        def _(z):
            for lo in range(0, rows, 16):
                at = pl.ds(lo, 16)
                held = phi[z, at, :]
                phi[z, at, :] = jnp.where(inside(z, lo, held.shape), held - 1.0, 0.0)

        z_lo, z_hi = MARGIN - 6, deep - (MARGIN - 6)

        def growth_piece(n):
            first_lo = SIDE - 8
            chunks = (own_y + 16) // 8
            span = z_hi - z_lo
            begin, end = z_lo + span * n // 3, z_lo + span * (n + 1) // 3

            @pl.loop(0, chunks)
            def _(c):
                at = pl.ds(pl.multiple_of(first_lo + 8 * c, 8), 8)
                along_planes(phi, gp, gm, begin, end, at)

            @pl.loop(begin, end)
            def _(z):
                plane_growth(phi, gp, gm, z, first_lo, chunks, first_lo, None)

        def take_halo(b):
            for dx in (-1, 1):
                @pl.when(has[(-dx, 0)])
                def _(dx=dx):
                    for l in range(3):
                        x_copy(dx, l, b).wait_recv()

            @pl.loop(0, fields)
            def _(f):
                for p in range(size_x, size_x + 3):
                    filter_rows(f, p, slice(8 * b, 8 * b + 8), (slice(8 * b + 8, 8 * b + 16),))

        def send_group(b):
            y = 8 * b

            @pl.loop(0, 3 * tiles)
            def _(k):
                march_planes(3 * (k // tiles), k % tiles, y, [size_x + 2, 0, 1, 2], [0])
                march_planes(
                    3 * (k // tiles), k % tiles, y,
                    [size_x - 3, size_x - 2, size_x - 1, size_x, size_x + 1], [size_x - 2, size_x - 1],
                )

            for t in range(tiles):
                parts = []
                for s in range(8):
                    at = pl.ds(y + s, size_x, stride=size_y)
                    parts.append(energy[t, at, :] * stiff[t, at, :])
                block = jnp.concatenate(parts, axis=0)
                top = jnp.max(block.reshape(block.shape[0] // 8, 8, 128), axis=0)
                peak_out[...] = jnp.maximum(peak_out[...], top)
                packed[b, MARGIN + 128 * t:MARGIN + 128 * (t + 1), :] = block.T

            pltpu.make_async_copy(
                packed.at[b, pl.ds(i * own_z, deep)], arrived.at[i, b + 2, pl.ds(0, deep)], a_sem.at[b]
            ).start()

            @pl.loop(1, wide)
            def _(k):
                w = (i + k) % wide
                remote(
                    packed.at[b, pl.ds(w * own_z, deep)], arrived.at[i, b + 2, pl.ds(0, deep)],
                    a_send.at[b, w], a_recv.at[b, i], w, j,
                ).start()

        for dx, dy in around[4:]:
            @pl.when(has[(-dx, -dy)])
            def _(dx=dx, dy=dy):
                c_copy(dx, dy).wait_recv()

        @pl.loop(0, fields)
        def _(f):
            for p in range(size_x, size_x + 3):
                filter_rows(f, p, slice(tail, tail + 8), tail_spots)

        take_halo(0)
        for b in range(groups):
            if b < groups - 1:
                take_halo(b + 1)
            send_group(b)
            if b < groups - 2:
                growth_piece(b)

        def wide_peak(k):
            w = (i + k) % wide
            return remote(peak_out, peak_in.at[i], p_send.at[w], p_recv.at[i], w, j)

        @pl.loop(1, wide)
        def _(k):
            wide_peak(k).start()

        def from_wide(k):
            s = (i + k) % wide
            return remote(peak_out, peak_in.at[s], p_send.at[s], p_recv.at[s], s, j)

        peak_mid[...] = peak_out[...]

        @pl.loop(1, wide)
        def _(k):
            from_wide(k).wait_recv()
            peak_mid[...] = jnp.maximum(peak_mid[...], peak_in[(i + k) % wide])

        def narrow_peak(k):
            n = (j + k) % narrow
            return remote(peak_mid, peak_all.at[j], n_send.at[n], n_recv.at[j], i, n)

        def from_narrow(k):
            s = (j + k) % narrow
            return remote(peak_mid, peak_all.at[s], n_send.at[s], n_recv.at[s], i, s)

        @pl.loop(1, narrow)
        def _(k):
            narrow_peak(k).start()

        for n in range(groups - 2, 3):
            growth_piece(n)

        def forward(b, s):
            near = -1 if b < 2 else 1
            slot = 6 + b if b < 2 else b - 2
            return near, remote(
                arrived.at[s, b + 2, pl.ds(0, deep)], arrived.at[s, slot, pl.ds(0, deep)], f_send.at[b, s], f_recv.at[b, s],
                i, j + near,
            )

        for b in range(groups):
            pltpu.make_async_copy(
                packed.at[b, pl.ds(i * own_z, deep)], arrived.at[i, b + 2, pl.ds(0, deep)], a_sem.at[b]
            ).wait()

            @pl.loop(0, wide)
            def _(k, b=b):
                s = (i + wide - k) % wide

                @pl.when(k > 0)
                def _():
                    remote(
                        packed.at[b, pl.ds(s * own_z, deep)], arrived.at[s, b + 2, pl.ds(0, deep)],
                        a_send.at[b, s], a_recv.at[b, s], s, j,
                    ).wait_recv()

                near = -1 if b < 2 else 1

                @pl.when(has[(0, near)])
                def _():
                    forward(b, s)[1].start()

        peak_all[j] = peak_mid[...]

        @pl.loop(1, narrow)
        def _(k):
            from_narrow(k).wait_recv()
            peak_all[j] = jnp.maximum(peak_all[j], peak_all[(j + k) % narrow])

        for b in range(groups):
            near = -1 if b < 2 else 1

            @pl.when(has[(0, -near)])
            def _(b=b):
                @pl.loop(0, wide)
                def _(s):
                    forward(b, s)[1].wait_recv()

        for b in range(groups):
            near = -1 if b < 2 else 1

            @pl.when(has[(0, near)])
            def _(b=b):
                @pl.loop(0, wide)
                def _(s):
                    forward(b, s)[1].wait_send()

            @pl.loop(1, wide)
            def _(k, b=b):
                w = (i + k) % wide
                remote(
                    packed.at[b, pl.ds(w * own_z, deep)], arrived.at[i, b + 2, pl.ds(0, deep)],
                    a_send.at[b, w], a_recv.at[b, i], w, j,
                ).wait_send()

        @pl.loop(1, wide)
        def _(k):
            wide_peak(k).wait_send()

        @pl.loop(1, narrow)
        def _(k):
            narrow_peak(k).wait_send()

        for dy in (-1, 1):
            @pl.when(has[(0, dy)])
            def _(dy=dy):
                for l in range(3):
                    y_copy(dy, l).wait_send()
        for dx in (-1, 1):
            @pl.when(has[(dx, 0)])
            def _(dx=dx):
                for l in range(3):
                    for b in range(groups):
                        x_copy(dx, l, b).wait_send()
        for dx, dy in around[4:]:
            @pl.when(has[(dx, dy)])
            def _(dx=dx, dy=dy):
                c_copy(dx, dy).wait_send()
        for k in range(8):
            @pl.when(has[around[k]])
            def _(k=k):
                lev_send_copy(k).wait_send()

    def plane_growth(source, gp, gm, z, start, chunks, rows_start, done):
        extra = 0 if rows_start == start else 1
        minus_parts, plus_parts = [], []
        for c in range(chunks + extra):
            minus, plus = along_rows(source, z, rows_start + 8 * c, 8)
            minus_parts.append(minus)
            plus_parts.append(plus)
        row = lax.broadcasted_iota(jnp.int32, (8, lanes), 0)
        for c in range(chunks):
            at = pl.ds(start + 8 * c, 8)
            if extra:
                low, here = minus_parts[c], minus_parts[c + 1]
                plus = plus_parts[c + 1]
            else:
                low, here = minus_parts[max(c - 1, 0)], minus_parts[c]
                plus = plus_parts[c]
            minus = jnp.where(row == 0, pltpu.roll(low, 1, 0), pltpu.roll(here, 1, 0))
            up_y, down_y = godunov(minus, plus)
            up_x, down_x = godunov(*along_lanes(source[z, at, :]))
            up = gp[z, at, :] + (up_y + up_x)
            down = gm[z, at, :] + (down_y + down_x)
            if done is None:
                gp[z, at, :] = jnp.sqrt(up)
                gm[z, at, :] = jnp.sqrt(down)
            else:
                done(z, at, c, up, down)

    def scoped(gp, gm):
        pl.run_scoped(
            lambda val, der: energy_phase(val, der, gp, gm),
            pltpu.VMEM((fields, size_x + 3, tiles, size_y + 16, 128), f32),
            pltpu.VMEM((fields, size_x + 3, tiles, size_y + 16, 128), f32),
        )
        pl.run_scoped(
            lambda *refs: march_phase(gp, gm, *refs),
            *[pltpu.VMEM(phi.shape, f32)] * 5,
        )

    def march_phase(gp, gm, psi, pull, keep, one, two):
        scale = jnp.max(peak_all[j]) + 1e-06
        flat = arrived.reshape(arrived.shape[0] * 8 * arrived.shape[2], 128)
        stride = 8 * arrived.shape[2]

        @pl.loop(0, deep)
        def _(z):
            for g in range(8):
                at = pl.ds(8 * g, 8)
                pieces = []
                for h in range(wide // 8):
                    first = h * 8 * stride + g * arrived.shape[2] + z
                    pieces.append(block_flip(flat[pl.ds(first, 8, stride=stride), :]))
                held = pieces[0] if len(pieces) == 1 else jnp.concatenate(pieces, axis=1)
                mask = inside(z, 8 * g, held.shape)
                velocity = jnp.where(mask, held / scale - 0.5, 0.0)
                level = phi[z, at, :] + 1.0
                weight = 1.0 / (1.0 + 4.0 * level * level)
                one[z, at, :] = velocity
                pull[z, at, :] = weight * velocity
                keep[z, at, :] = jnp.where(mask, (1.0 - weight) * (1.0 / 6.0), 0.0)

        source, target = one, two
        lane = lax.broadcasted_iota(jnp.int32, (8, lanes), 1)
        for step in range(EXT_PASSES):
            margin = MARGIN - 1 - step
            if step == 0:
                lo, chunks = SIDE - 12, (own_y + 24) // 8
            else:
                lo, chunks = SIDE - 8, (own_y + 16) // 8
            last = step == EXT_PASSES - 1

            def extend(z, source=source, target=target, lo=lo, chunks=chunks, last=last):
                for c in range(chunks):
                    start = lo + 8 * c
                    at = pl.ds(start, 8)
                    mid = source[z, at, :]
                    total = source[z - 1, at, :] + source[z + 1, at, :]
                    total = total + (source[z, pl.ds(start - 1, 8), :] + source[z, pl.ds(start + 1, 8), :])
                    low = jnp.where(lane == 0, 0.0, pltpu.roll(mid, 1, 1))
                    high = jnp.where(lane == lanes - 1, 0.0, pltpu.roll(mid, lanes - 1, 1))
                    value = pull[z, at, :] + keep[z, at, :] * (total + (low + high))
                    target[z, at, :] = value
                    if last:
                        growth = jnp.where(value > 0.0, gp[z, at, :], gm[z, at, :])
                        psi[z, at, :] = phi[z, at, :] - (TIME_STEP / 6.0) * (value * growth)

            pl.loop(step + 1, deep - step - 1)(extend)
            source, target = target, source
        speed = source

        source, target = psi, phi
        for step in range(1, HJ_STEPS):
            margin = 3 * (HJ_STEPS - 1 - step)
            final = step == HJ_STEPS - 1
            z_lo, z_hi = MARGIN - margin, MARGIN + own_z + margin
            if final:
                lo, chunks = SIDE, own_y // 8
            elif lanes == 128:
                lo, chunks = SIDE - 4, (own_y + 8) // 8
            else:
                lo, chunks = SIDE - 8, (own_y + 16) // 8
            unit = 8 if lo % 8 == 0 else 4

            @pl.loop(0, chunks)
            def _(c, source=source, lo=lo, unit=unit, z_lo=z_lo, z_hi=z_hi):
                along_planes(source, gp, gm, z_lo, z_hi, pl.ds(pl.multiple_of(lo + 8 * c, unit), 8))

            def done(z, at, c, up, down, source=source, target=target, final=final):
                rate = speed[z, at, :]
                growth = jnp.sqrt(jnp.where(rate > 0.0, up, down))
                value = source[z, at, :] - (TIME_STEP / 6.0) * (rate * growth)
                if final:
                    next_ref[z - MARGIN, pl.ds(8 * c, 8), :] = value + 1.0
                    speed_ref[z - MARGIN, pl.ds(8 * c, 8), :] = rate
                else:
                    target[z, at, :] = value

            rows_start = lo - 8 if final else lo

            @pl.loop(z_lo, z_hi)
            def _(z, source=source, lo=lo, chunks=chunks, rows_start=rows_start, done=done):
                plane_growth(source, gp, gm, z, lo, chunks, rows_start, done)

            source, target = target, source

    pl.run_scoped(scoped, pltpu.VMEM(phi.shape, f32), pltpu.VMEM(phi.shape, f32))


def per_device(displacement, material, level_set, wide, narrow):
    own_z, own_y, lanes = level_set.shape
    loads, comps, size_x, size_y, size_z = displacement.shape
    fields = loads * comps
    deep = own_z + 2 * MARGIN
    groups = own_y // 8
    tiles = size_z // 128
    padded = -(-(size_z + 2 * MARGIN) // 8) * 8
    result = jax.ShapeDtypeStruct((own_z, own_y, lanes), f32)
    dma = pltpu.SemaphoreType.DMA
    vmem = pl.BlockSpec(memory_space=pltpu.VMEM)
    hbm = pl.BlockSpec(memory_space=pl.ANY)
    return pl.pallas_call(
        functools.partial(kernel, wide=wide, narrow=narrow),
        out_shape=(result, result),
        in_specs=[hbm, vmem, hbm],
        out_specs=(vmem, vmem),
        scratch_shapes=[
            pltpu.VMEM((fields, size_x + 3, size_y + 8, size_z), f32),
            pltpu.VMEM((tiles, size_x * size_y, 128), f32),
            pltpu.VMEM((tiles, size_x * size_y, 128), f32),
            pltpu.VMEM((groups, padded, 128), f32),
            pltpu.VMEM((wide, 8, -(-deep // 8) * 8, 128), f32),
            pltpu.VMEM((deep, own_y + 2 * SIDE, lanes), f32),
            pltpu.VMEM((8, 128), f32),
            pltpu.VMEM((wide, 8, 128), f32),
            pltpu.VMEM((8, 128), f32),
            pltpu.VMEM((narrow, 8, 128), f32),
            dma((3,)), dma((2, 3, groups)), dma((2, 3, groups)), dma((2, 3)), dma((2, 3)), dma((4,)), dma((4,)),
            dma, dma((8,)), dma((8,)),
            dma((groups,)), dma((groups, wide)), dma((groups, wide)),
            dma((groups, wide)), dma((groups, wide)),
            dma((wide,)), dma((wide,)), dma((narrow,)), dma((narrow,)),
        ],
        compiler_params=pltpu.CompilerParams(
            vmem_limit_bytes=62 << 20, collective_id=0, has_side_effects=True
        ),
    )(
        displacement.reshape(fields, size_x, size_y, size_z),
        material.reshape(size_x * size_y, material.shape[2]),
        level_set,
    )


def solution(mesh):
    return jax.shard_map(
        functools.partial(per_device, wide=mesh.shape["wide"], narrow=mesh.shape["narrow"]),
        mesh=mesh,
        in_specs=(
            P(None, None, "wide", "narrow", None),
            P("wide", "narrow", None),
            P("wide", "narrow", None),
        ),
        out_specs=(P("wide", "narrow", None), P("wide", "narrow", None)),
        check_vma=False,
    )
```

```python
import functools

import jax
import jax.numpy as jnp
from jax import lax
from jax.experimental import pallas as pl
from jax.experimental.pallas import tpu as pltpu
from jax.sharding import PartitionSpec as P

BZ = 16
EXT_PASSES = 4
HJ_STEPS = 3
SHEAR = 0.384615
LAME = 0.576923
WENO_EPS = 1e-06
TIME_STEP = 0.3
TAP_SCALE = 1.0 / (48.0 * 48.0 * 8.0)
MARGIN = EXT_PASSES
SIDE = 8
REACH = 3
MESH = pl.DeviceIdType.MESH
f32 = jnp.float32


def val_taps(a, b, c, d):
    return (a + d) + 23.0 * (b + c)


def der_taps(a, b, c, d):
    return (d - a) + 5.0 * (c - b)


def z_filters(u):
    size = u.shape[-1]
    rows = u.shape[0]
    lane = lax.broadcasted_iota(jnp.int32, (rows, 128), 1)
    count = size // 128
    tiles = [u[:, t * 128:(t + 1) * 128] for t in range(count)]
    zero = jnp.zeros((rows, 128), f32)
    up = [pltpu.roll(t, 1, 1) for t in tiles]
    one = [pltpu.roll(t, 127, 1) for t in tiles] + [zero]
    two = [pltpu.roll(t, 126, 1) for t in tiles] + [zero]
    vals, ders = [], []
    for t in range(count):
        before = jnp.where(lane == 0, up[t - 1] if t else zero, up[t])
        after = jnp.where(lane == 127, one[t + 1], one[t])
        second = jnp.where(lane >= 126, two[t + 1], two[t])
        vals.append(val_taps(before, tiles[t], after, second))
        ders.append(der_taps(before, tiles[t], after, second))
    return vals, ders


def minus_side(e0, e1, t0, t1, c1, c3, p, q6, r3):
    low = p * (e0 + (c1 + c1)) + q6 * (e0 + t1) + r3 * (t1 + c3)
    return low, (p + q6) + r3


def plus_side(e0, e1, t0, t1, c1, c3, r, q6, p3):
    high = r * (e1 + (c3 + c3)) + q6 * (e1 + t0) + p3 * (t0 + c1)
    return high, (r + q6) + p3


EPS = 0.75 * WENO_EPS


def both_sides(d6, e0, e1, s0, s2, q0, q1, q2, g0, g1, t0, t1):
    c1 = e0 + s0
    c3 = e1 - s2
    a = q0 + g0 * c1
    b = q1 + g0 * e1
    c = q2 + g1 * c3
    a, b, c = a * a, b * b, c * c
    p, q6, r = b * c, 6.0 * (a * c), a * b
    low, low_sum = minus_side(e0, e1, t0, t1, c1, c3, p, q6, 3.0 * r)
    high, high_sum = plus_side(e0, e1, t0, t1, c1, c3, r, q6, 3.0 * p)
    return d6 + low / low_sum, high / high_sum - d6


def godunov(minus, plus):
    up = jnp.maximum(jnp.maximum(minus, plus), 0.0)
    down = jnp.minimum(jnp.minimum(minus, plus), 0.0)
    return up * up, down * down


def along_lanes(mid):
    size = mid.shape[-1]
    lane = lax.broadcasted_iota(jnp.int32, mid.shape, 1)
    u = []
    for k in range(-3, 4):
        if k == 0:
            u.append(mid)
            continue
        moved = pltpu.roll(mid, (-k) % size, 1)
        u.append(jnp.where(lane < -k if k < 0 else lane >= size - k, 0.0, moved))
    d = [u[k + 1] - u[k] for k in range(6)]
    e0, e1, e2, e3, e4 = [d[k + 1] - d[k] for k in range(5)]
    s = [e1 - e0, e2 - e1, e3 - e2, e4 - e3]
    q = [x * x + EPS for x in s]
    g = [0.75 * x for x in (e1, e2, e3)]
    t = [x + x for x in (e1, e2, e3)]
    c1, c3 = e1 + s[0], e2 - s[2]
    a, b, c = q[0] + g[0] * c1, q[1] + g[0] * e2, q[2] + g[1] * c3
    a, b, c = a * a, b * b, c * c
    low, low_sum = minus_side(e1, e2, t[0], t[1], c1, c3, b * c, 6.0 * (a * c), 3.0 * (a * b))
    c1, c3 = e2 + s[1], e3 - s[3]
    a, b, c = q[1] + g[1] * c1, q[2] + g[1] * e3, q[3] + g[2] * c3
    a, b, c = a * a, b * b, c * c
    high, high_sum = plus_side(e2, e3, t[1], t[2], c1, c3, a * b, 6.0 * (a * c), 3.0 * (b * c))
    return 6.0 * d[2] + low / low_sum, high / high_sum - 6.0 * d[3]


def along_rows(ref, z, start, count):
    u = [ref[z, pl.ds(start + k, count), :] for k in range(-2, 4)]
    d = [u[k + 1] - u[k] for k in range(5)]
    e = [d[k + 1] - d[k] for k in range(4)]
    s = [e[k + 1] - e[k] for k in range(3)]
    q = [x * x + EPS for x in s]
    return both_sides(
        6.0 * d[2], e[1], e[2], s[0], s[2], q[0], q[1], q[2], 0.75 * e[1], 0.75 * e[2], e[1] + e[1], e[2] + e[2]
    )


def along_planes(ref, gp, gm, z_lo, z_hi, at):
    u = [ref[z_lo - 3 + k, at, :] for k in range(5)]
    d = [u[k + 1] - u[k] for k in range(4)]
    e = [d[k + 1] - d[k] for k in range(3)]
    s = [e[k + 1] - e[k] for k in range(2)]
    q = [x * x + EPS for x in s]
    g = 0.75 * e[1]
    t = e[1] + e[1]
    newest, d_mid, d_new = u[4], d[2], d[3]
    behind = None
    for z in range(z_lo - 1, z_hi):
        plane = ref[z + 3, at, :]
        d_next = plane - newest
        e_next = d_next - d_new
        s_next = e_next - e[2]
        q_next = s_next * s_next + EPS
        g_next = 0.75 * e[2]
        t_next = e[2] + e[2]
        minus, plus = both_sides(
            6.0 * d_mid, e[1], e[2], s[0], s_next, q[0], q[1], q_next, g, g_next, t, t_next
        )
        if behind is not None:
            up, down = godunov(behind, plus)
            gp[z, at, :] = up
            gm[z, at, :] = down
        behind = minus
        newest, d_mid, d_new = plane, d_new, d_next
        e = [e[1], e[2], e_next]
        s = [s[1], s_next]
        q = [q[1], q_next]
        g, t = g_next, t_next


def block_flips(blocks):
    row = lax.broadcasted_iota(jnp.int32, (8, 128), 0)
    part = lax.broadcasted_iota(jnp.int32, (8, 128), 1) // 16
    far = [pltpu.roll(x, 4, 0) for x in blocks]
    far = [pltpu.roll(x, 64, 1) for x in far]
    same = (row // 4) % 2 == (part // 4) % 2
    blocks = [jnp.where(same, x, y) for x, y in zip(blocks, far)]
    for bit in (2, 1):
        row_bit, part_bit = (row // bit) % 2, (part // bit) % 2
        down = [pltpu.roll(x, bit, 0) for x in blocks]
        up = [pltpu.roll(x, 8 - bit, 0) for x in blocks]
        down = [pltpu.roll(x, 128 - 16 * bit, 1) for x in down]
        up = [pltpu.roll(x, 16 * bit, 1) for x in up]
        same, below = row_bit == part_bit, row_bit > part_bit
        blocks = [jnp.where(same, x, jnp.where(below, y, z)) for x, y, z in zip(blocks, down, up)]
    return blocks


def kernel(
    disp, mat, lev, next_ref, speed_ref,
    field, energy, stiff, packed, arrived, phi, psi, peak_out, peak_in, peak_mid, peak_all,
    own_sem, x_send, x_recv, y_send, y_recv, c_send, c_recv, lev_sem, lev_send, lev_recv,
    a_sem, a_send, a_recv, f_send, f_recv, p_send, p_recv, n_send, n_recv, e_send, e_recv,
    *, wide, narrow,
):
    i = lax.axis_index("wide")
    j = lax.axis_index("narrow")
    fields, size_x, size_y, size_z = disp.shape
    own_z, own_y, lanes = lev.shape
    deep, rows, _ = phi.shape
    tiles = size_z // 128
    groups = own_y // 8
    tail = size_y
    reach_y = REACH if lanes == 128 else SIDE
    slots = groups + 2
    has = {(-1, 0): i > 0, (1, 0): i < wide - 1, (0, -1): j > 0, (0, 1): j < narrow - 1}
    for a in (-1, 1):
        for b in (-1, 1):
            has[(a, b)] = has[(a, 0)] & has[(0, b)]
    around = [(-1, 0), (1, 0), (0, -1), (0, 1), (-1, -1), (-1, 1), (1, -1), (1, 1)]

    def remote(src, dst, send, recv, w, n):
        return pltpu.make_async_remote_copy(
            src_ref=src, dst_ref=dst, send_sem=send, recv_sem=recv,
            device_id={"wide": w, "narrow": n}, device_id_type=MESH,
        )

    own_copies = [
        pltpu.make_async_copy(
            disp.at[3 * l:3 * l + 3], field.at[3 * l:3 * l + 3, 0:size_x, 0:size_y], own_sem.at[l]
        )
        for l in range(3)
    ]
    lev_copy = pltpu.make_async_copy(
        lev, phi.at[MARGIN:MARGIN + own_z, SIDE:SIDE + own_y], lev_sem
    )

    def plane_part(dx):
        if dx < 0:
            return slice(0, 2), slice(size_x, size_x + 2)
        if dx > 0:
            return slice(size_x - 1, size_x), slice(size_x + 2, size_x + 3)
        return slice(0, size_x), slice(0, size_x)

    def row_part(dy):
        if dy < 0:
            return slice(0, 2), slice(tail, tail + 2)
        return slice(size_y - 1, size_y), slice(tail + 7, tail + 8)

    def x_copy(dx, l, b):
        src, dst = plane_part(dx)
        at = slice(8 * b, 8 * b + 8)
        k = (dx + 1) // 2
        return remote(
            disp.at[3 * l:3 * l + 3, src, at], field.at[3 * l:3 * l + 3, dst, at],
            x_send.at[k, l, b], x_recv.at[k, l, b], i + dx, j,
        )

    def y_copy(dy, l):
        src, dst = row_part(dy)
        k = (dy + 1) // 2
        return remote(
            disp.at[3 * l:3 * l + 3, :, src], field.at[3 * l:3 * l + 3, 0:size_x, dst],
            y_send.at[k, l], y_recv.at[k, l], i, j + dy,
        )

    def c_copy(dx, dy):
        xs, xd = plane_part(dx)
        ys, yd = row_part(dy)
        k = (dx + 1) + (dy + 1) // 2
        return remote(
            disp.at[:, xs, ys], field.at[:, xd, yd], c_send.at[k], c_recv.at[k], i + dx, j + dy
        )

    def lev_part(step, size, width, before):
        if step < 0:
            return slice(0, width), slice(before + size, before + size + width)
        if step > 0:
            return slice(size - width, size), slice(before - width, before)
        return slice(0, size), slice(before, before + size)

    def lev_send_copy(k):
        dx, dy = around[k]
        zs, zd = lev_part(dx, own_z, REACH, MARGIN)
        ys, yd = lev_part(dy, own_y, reach_y, SIDE)
        return remote(lev.at[zs, ys], phi.at[zd, yd], lev_send.at[k], lev_recv.at[k], i + dx, j + dy)

    def step_copy(n, ref, k):
        dx, dy = around[k]
        zs, zd = lev_part(dx, own_z, REACH, 0)
        ys, yd = lev_part(dy, own_y, reach_y, 0)

        def tile(z, y):
            return ref.at[slice(z.start + MARGIN, z.stop + MARGIN), slice(y.start + SIDE, y.stop + SIDE)]

        return remote(tile(zs, ys), tile(zd, yd), e_send.at[n, k], e_recv.at[n, k], i + dx, j + dy)

    def step_do(n, ref, k, what):
        dx, dy = around[k]
        sign = -1 if what == "wait_recv" else 1

        @pl.when(has[(sign * dx, sign * dy)])
        def _():
            getattr(step_copy(n, ref, k), what)()

    for copy in own_copies:
        copy.start()
    lev_copy.start()

    barrier = pltpu.get_barrier_semaphore()

    @pl.loop(1, wide)
    def _(k):
        pl.semaphore_signal(
            barrier, inc=1, device_id={"wide": (i + k) % wide, "narrow": j}, device_id_type=MESH
        )

    @pl.loop(1, narrow)
    def _(k):
        pl.semaphore_signal(
            barrier, inc=1, device_id={"wide": i, "narrow": (j + k) % narrow}, device_id_type=MESH
        )

    for dx, dy in around[4:]:
        @pl.when(has[(dx, dy)])
        def _(dx=dx, dy=dy):
            pl.semaphore_signal(
                barrier, inc=1, device_id={"wide": i + dx, "narrow": j + dy}, device_id_type=MESH
            )
    beside_x = jnp.where(i > 0, 1, 0) + jnp.where(i < wide - 1, 1, 0)
    beside_y = jnp.where(j > 0, 1, 0) + jnp.where(j < narrow - 1, 1, 0)
    pl.semaphore_wait(barrier, wide - 1 + narrow - 1 + beside_x * beside_y)

    for dy in (-1, 1):
        @pl.when(has[(0, dy)])
        def _(dy=dy):
            for l in range(3):
                y_copy(dy, l).start()
    for b in range(groups):
        for dx in (-1, 1):
            @pl.when(has[(dx, 0)])
            def _(dx=dx, b=b):
                for l in range(3):
                    x_copy(dx, l, b).start()
        if b == 0:
            for dx, dy in around[4:]:
                @pl.when(has[(dx, dy)])
                def _(dx=dx, dy=dy):
                    c_copy(dx, dy).start()
            for k in range(8):
                @pl.when(has[around[k]])
                def _(k=k):
                    lev_send_copy(k).start()

    for dx, planes in ((1, (size_x, size_x + 1)), (-1, (size_x + 2,))):
        @pl.when(jnp.logical_not(has[(dx, 0)]))
        def _(planes=planes):
            @pl.loop(0, fields)
            def _(f):
                for p in planes:
                    field[f, p] = jnp.zeros(field.shape[2:], f32)

    for dy, lo, hi in ((1, tail, tail + 2), (-1, tail + 7, tail + 8)):
        @pl.when(jnp.logical_not(has[(0, dy)]))
        def _(lo=lo, hi=hi):
            @pl.loop(0, fields)
            def _(f):
                for p in range(size_x + 3):
                    field[f, p, lo:hi, :] = jnp.zeros((hi - lo, size_z), f32)

    block = lax.broadcasted_iota(jnp.int32, (mat.shape[1], size_z), 0)
    column = lax.broadcasted_iota(jnp.int32, (mat.shape[1], size_z), 1) // BZ
    spread = jnp.where(block == column, 1.0, 0.0)

    @pl.loop(0, size_x)
    def _(p):
        solid = lax.dot_general(
            mat[p].astype(f32), spread, (((0,), (0,)), ((), ())), preferred_element_type=f32
        )
        for t in range(tiles):
            at = pl.ds(pl.multiple_of(p * size_y, 8), size_y)
            stiff[t, at, :] = 0.2 + 0.8 * solid[:, t * 128:(t + 1) * 128]
            energy[t, at, :] = jnp.zeros((size_y, 128), f32)

    for b in range(groups):
        packed[b] = jnp.zeros(packed.shape[1:], f32)
    peak_out[...] = jnp.zeros(peak_out.shape, f32)

    @pl.loop(0, deep)
    def _(z):
        psi[z] = jnp.zeros(psi.shape[1:], f32)

    def inside(z, lo, shape):
        here = i * own_z - MARGIN + z
        row = lax.broadcasted_iota(jnp.int32, shape, 0) + (lo + j * own_y - SIDE)
        end = narrow * own_y
        lowest = jnp.where((here >= 0) & (here < wide * own_z), 0, end)
        return (row >= lowest) & (row < end)

    def energy_phase(val, der, gp, gm):
        def filter_rows(f, p, at, spots):
            vals, ders = z_filters(field[f, p, at, :])
            for t in range(tiles):
                for spot in spots:
                    val[f, p, t, spot, :] = vals[t]
                    der[f, p, t, spot, :] = ders[t]

        tail_spots = (slice(0, 8), slice(8 + size_y, 16 + size_y))

        for l in range(3):
            own_copies[l].wait()

            @pl.loop(0, 3 * size_x // 2)
            def _(k, l=l):
                for p in range(2):
                    filter_rows(
                        3 * l + (2 * k) // size_x, (2 * k) % size_x + p, slice(0, size_y),
                        (slice(8, 8 + size_y),),
                    )

        for dy in (-1, 1):
            @pl.when(has[(0, -dy)])
            def _(dy=dy):
                for l in range(3):
                    y_copy(dy, l).wait_recv()

        @pl.loop(0, fields)
        def _(f):
            for p in range(size_x):
                filter_rows(f, p, slice(tail, tail + 8), tail_spots)

        def march_planes(f, t, y, planes, out):
            held = []
            for n, p in enumerate(planes):
                v = [[val[f + c, p, t, pl.ds(y + 7 + k, 8), :] for k in range(4)] for c in range(3)]
                w = [[der[f + c, p, t, pl.ds(y + 7 + k, 8), :] for k in range(4)] for c in range(3)]
                vv = [val_taps(*x) for x in v]
                vd = [der_taps(*x) for x in v]
                dv = [val_taps(*x) for x in w]
                held.append((vv[0], vd[0], dv[0], vv[1], vd[1], vv[2], dv[2], dv[1] + vd[2]))
                if len(held) < 4:
                    continue
                line = list(zip(*held))
                held = held[1:]
                exx = der_taps(*line[0])
                eyy = val_taps(*line[4])
                ezz = val_taps(*line[6])
                exy = val_taps(*line[1]) + der_taps(*line[3])
                exz = val_taps(*line[2]) + der_taps(*line[5])
                eyz = val_taps(*line[7])
                trace = exx + eyy + ezz
                square = (exx * exx + eyy * eyy + ezz * ezz) + 0.5 * (exy * exy + exz * exz + eyz * eyz)
                density = (SHEAR * TAP_SCALE * TAP_SCALE) * square
                density = density + (0.5 * LAME * TAP_SCALE * TAP_SCALE) * (trace * trace)
                at = pl.ds(out[n - 3] * size_y + y, 8)
                energy[t, at, :] = energy[t, at, :] + density

        @pl.loop(0, 3 * tiles * groups)
        def _(k):
            y = pl.multiple_of((k % groups) * 8, 8)
            march_planes(
                3 * (k // (tiles * groups)), (k // groups) % tiles, y,
                list(range(size_x)), list(range(1, size_x - 2)),
            )

        lev_copy.wait()
        for k in range(8):
            dx, dy = around[k]

            @pl.when(has[(-dx, -dy)])
            def _(k=k):
                lev_send_copy(k).wait_recv()

        @pl.loop(0, deep)
        def _(z):
            for lo in range(0, rows, 16):
                at = pl.ds(lo, 16)
                held = phi[z, at, :]
                phi[z, at, :] = jnp.where(inside(z, lo, held.shape), held - 1.0, 0.0)

        def growth_piece(n):
            begin, end = MARGIN + own_z * n // 3, MARGIN + own_z * (n + 1) // 3

            @pl.loop(0, groups)
            def _(c):
                along_planes(phi, gp, gm, begin, end, pl.ds(pl.multiple_of(SIDE + 8 * c, 8), 8))

            plane_growth(phi, gp, gm, begin, end, None)

        def take_halo(b):
            for dx in (-1, 1):
                @pl.when(has[(-dx, 0)])
                def _(dx=dx):
                    for l in range(3):
                        x_copy(dx, l, b).wait_recv()

            @pl.loop(0, fields)
            def _(f):
                for p in range(size_x, size_x + 3):
                    filter_rows(f, p, slice(8 * b, 8 * b + 8), (slice(8 * b + 8, 8 * b + 16),))

        def send_group(b):
            y = 8 * b

            @pl.loop(0, 3 * tiles)
            def _(k):
                march_planes(3 * (k // tiles), k % tiles, y, [size_x + 2, 0, 1, 2], [0])
                march_planes(
                    3 * (k // tiles), k % tiles, y,
                    [size_x - 3, size_x - 2, size_x - 1, size_x, size_x + 1], [size_x - 2, size_x - 1],
                )

            for t in range(tiles):
                parts = []
                for s in range(8):
                    at = pl.ds(y + s, size_x, stride=size_y)
                    parts.append(energy[t, at, :] * stiff[t, at, :])
                block = jnp.concatenate(parts, axis=0)
                top = jnp.max(block.reshape(block.shape[0] // 8, 8, 128), axis=0)
                peak_out[...] = jnp.maximum(peak_out[...], top)
                packed[b, MARGIN + 128 * t:MARGIN + 128 * (t + 1), :] = block.T

            pltpu.make_async_copy(
                packed.at[b, pl.ds(i * own_z, deep)], arrived.at[i, b + 1, pl.ds(0, deep)], a_sem.at[b]
            ).start()

            @pl.loop(1, wide)
            def _(k):
                w = (i + k) % wide
                remote(
                    packed.at[b, pl.ds(w * own_z, deep)], arrived.at[i, b + 1, pl.ds(0, deep)],
                    a_send.at[b, w], a_recv.at[b, i], w, j,
                ).start()

        for dx, dy in around[4:]:
            @pl.when(has[(-dx, -dy)])
            def _(dx=dx, dy=dy):
                c_copy(dx, dy).wait_recv()

        @pl.loop(0, fields)
        def _(f):
            for p in range(size_x, size_x + 3):
                filter_rows(f, p, slice(tail, tail + 8), tail_spots)

        take_halo(0)
        for b in range(groups):
            if b < groups - 1:
                take_halo(b + 1)
            send_group(b)
            if b < groups - 2:
                growth_piece(b)

        def wide_peak(k):
            w = (i + k) % wide
            return remote(peak_out, peak_in.at[i], p_send.at[w], p_recv.at[i], w, j)

        @pl.loop(1, wide)
        def _(k):
            wide_peak(k).start()

        def from_wide(k):
            s = (i + k) % wide
            return remote(peak_out, peak_in.at[s], p_send.at[s], p_recv.at[s], s, j)

        peak_mid[...] = peak_out[...]

        @pl.loop(1, wide)
        def _(k):
            from_wide(k).wait_recv()
            peak_mid[...] = jnp.maximum(peak_mid[...], peak_in[(i + k) % wide])

        def narrow_peak(k):
            n = (j + k) % narrow
            return remote(peak_mid, peak_all.at[j], n_send.at[n], n_recv.at[j], i, n)

        def from_narrow(k):
            s = (j + k) % narrow
            return remote(peak_mid, peak_all.at[s], n_send.at[s], n_recv.at[s], i, s)

        @pl.loop(1, narrow)
        def _(k):
            narrow_peak(k).start()

        for n in range(groups - 2, 3):
            growth_piece(n)

        passed = ((0, -1, slots - 1), (groups - 1, 1, 0))

        def forward(n, s):
            b, near, slot = passed[n]
            return remote(
                arrived.at[s, b + 1, pl.ds(0, deep)], arrived.at[s, slot, pl.ds(0, deep)],
                f_send.at[n, s], f_recv.at[n, s], i, j + near,
            )

        for b in range(groups):
            pltpu.make_async_copy(
                packed.at[b, pl.ds(i * own_z, deep)], arrived.at[i, b + 1, pl.ds(0, deep)], a_sem.at[b]
            ).wait()

            @pl.loop(0, wide)
            def _(k, b=b):
                s = (i + wide - k) % wide

                @pl.when(k > 0)
                def _():
                    remote(
                        packed.at[b, pl.ds(s * own_z, deep)], arrived.at[s, b + 1, pl.ds(0, deep)],
                        a_send.at[b, s], a_recv.at[b, s], s, j,
                    ).wait_recv()

                for n in range(2):
                    if passed[n][0] == b:
                        @pl.when(has[(0, passed[n][1])])
                        def _(n=n):
                            forward(n, s).start()

        peak_all[j] = peak_mid[...]

        @pl.loop(1, narrow)
        def _(k):
            from_narrow(k).wait_recv()
            peak_all[j] = jnp.maximum(peak_all[j], peak_all[(j + k) % narrow])

        for n in range(2):
            @pl.when(has[(0, -passed[n][1])])
            def _(n=n):
                @pl.loop(0, wide)
                def _(s):
                    forward(n, s).wait_recv()

        for n in range(2):
            @pl.when(has[(0, passed[n][1])])
            def _(n=n):
                @pl.loop(0, wide)
                def _(s):
                    forward(n, s).wait_send()

        for b in range(groups):
            @pl.loop(1, wide)
            def _(k, b=b):
                w = (i + k) % wide
                remote(
                    packed.at[b, pl.ds(w * own_z, deep)], arrived.at[i, b + 1, pl.ds(0, deep)],
                    a_send.at[b, w], a_recv.at[b, i], w, j,
                ).wait_send()

        @pl.loop(1, wide)
        def _(k):
            wide_peak(k).wait_send()

        @pl.loop(1, narrow)
        def _(k):
            narrow_peak(k).wait_send()

        for dy in (-1, 1):
            @pl.when(has[(0, dy)])
            def _(dy=dy):
                for l in range(3):
                    y_copy(dy, l).wait_send()
        for dx in (-1, 1):
            @pl.when(has[(dx, 0)])
            def _(dx=dx):
                for l in range(3):
                    for b in range(groups):
                        x_copy(dx, l, b).wait_send()
        for dx, dy in around[4:]:
            @pl.when(has[(dx, dy)])
            def _(dx=dx, dy=dy):
                c_copy(dx, dy).wait_send()
        for k in range(8):
            @pl.when(has[around[k]])
            def _(k=k):
                lev_send_copy(k).wait_send()

    def plane_growth(source, gp, gm, begin, end, done):
        if end <= begin:
            return
        row = lax.broadcasted_iota(jnp.int32, (8, lanes), 0)
        batch = 2 if (end - begin) % 2 == 0 else 1

        def one_plane(z):
            before, _ = along_rows(source, z, SIDE - 4, 8)
            before = pltpu.roll(before, 5, 0)
            for c in range(groups):
                at = pl.ds(SIDE + 8 * c, 8)
                here, plus = along_rows(source, z, SIDE + 8 * c, 8)
                moved = pltpu.roll(here, 1, 0)
                up_y, down_y = godunov(jnp.where(row == 0, before, moved), plus)
                before = moved
                up_x, down_x = godunov(*along_lanes(source[z, at, :]))
                up = gp[z, at, :] + (up_y + up_x)
                down = gm[z, at, :] + (down_y + down_x)
                if done is None:
                    gp[z, at, :] = jnp.sqrt(up)
                    gm[z, at, :] = jnp.sqrt(down)
                else:
                    done(z, at, c, up, down)

        @pl.loop(0, (end - begin) // batch)
        def _(k):
            for r in range(batch):
                one_plane(begin + batch * k + r)

    def scoped(gp, gm):
        pl.run_scoped(
            lambda val, der: energy_phase(val, der, gp, gm),
            pltpu.VMEM((fields, size_x + 3, tiles, size_y + 16, 128), f32),
            pltpu.VMEM((fields, size_x + 3, tiles, size_y + 16, 128), f32),
        )
        pl.run_scoped(
            lambda *refs: march_phase(gp, gm, *refs),
            *[pltpu.VMEM(phi.shape, f32)] * 4,
        )

    def most(count, options):
        return next(n for n in options if count % n == 0)

    def march_phase(gp, gm, pull, keep, one, two):
        scale = jnp.max(peak_all[j]) + 1e-06
        flat = arrived.reshape(arrived.shape[0] * slots * arrived.shape[2], 128)
        stride = slots * arrived.shape[2]
        batch = most(deep, (2, 1))

        @pl.loop(0, deep // batch)
        def _(k):
            raw = []
            for r in range(batch):
                for g in range(slots):
                    for h in range(wide // 8):
                        first = h * 8 * stride + g * arrived.shape[2] + batch * k + r
                        raw.append(flat[pl.ds(first, 8, stride=stride), :])
            raw = block_flips(raw)
            for r in range(batch):
                z = batch * k + r
                for g in range(slots):
                    at = pl.ds(8 * g, 8)
                    pieces = [raw.pop(0) for _ in range(wide // 8)]
                    held = pieces[0] if len(pieces) == 1 else jnp.concatenate(pieces, axis=1)
                    mask = inside(z, 8 * g, held.shape)
                    velocity = jnp.where(mask, held / scale - 0.5, 0.0)
                    level = phi[z, at, :] + 1.0
                    weight = 1.0 / (1.0 + 4.0 * level * level)
                    one[z, at, :] = velocity
                    pull[z, at, :] = weight * velocity
                    keep[z, at, :] = jnp.where(mask, (1.0 - weight) * (1.0 / 6.0), 0.0)

        top, bottom = MARGIN, MARGIN + own_z
        edge = 6
        source, target = one, two
        lane = lax.broadcasted_iota(jnp.int32, (8, lanes), 1)
        for step in range(EXT_PASSES):
            last = step == EXT_PASSES - 1
            lo, chunks = (SIDE, groups) if last else (SIDE - 4, groups + 1)

            def extend(planes, source=source, target=target, lo=lo, chunks=chunks, last=last):
                spots = [(z, lo + 8 * c) for z in planes for c in range(chunks)]
                mids = [source[z, pl.ds(start, 8), :] for z, start in spots]
                lows = [pltpu.roll(mid, 1, 1) for mid in mids]
                highs = [pltpu.roll(mid, lanes - 1, 1) for mid in mids]
                for (z, start), low, high in zip(spots, lows, highs):
                    at = pl.ds(start, 8)
                    total = source[z - 1, at, :] + source[z + 1, at, :]
                    total = total + (source[z, pl.ds(start - 1, 8), :] + source[z, pl.ds(start + 1, 8), :])
                    low = jnp.where(lane == 0, 0.0, low)
                    high = jnp.where(lane == lanes - 1, 0.0, high)
                    value = pull[z, at, :] + keep[z, at, :] * (total + (low + high))
                    target[z, at, :] = value
                    if last:
                        growth = jnp.where(value > 0.0, gp[z, at, :], gm[z, at, :])
                        psi[z, at, :] = phi[z, at, :] - (TIME_STEP / 6.0) * (value * growth)

            def extend_all(begin, end, extend=extend):
                if end <= begin:
                    return
                size = most(end - begin, (6, 5, 4, 3, 2, 1))

                @pl.loop(0, (end - begin) // size)
                def _(k):
                    extend([begin + size * k + r for r in range(size)])

            if last:
                extend_all(top, top + edge)
                extend_all(bottom - edge, bottom)
                step_do(0, psi, 0, "start")
                extend_all(top + edge, bottom - edge)
                step_do(0, psi, 1, "start")
            else:
                extend_all(step + 1, deep - step - 1)
            source, target = target, source
        speed = source

        source, target = psi, phi
        for step in range(1, HJ_STEPS):
            final = step == HJ_STEPS - 1

            def planes_of(begin, end, c, source=source):
                along_planes(source, gp, gm, begin, end, pl.ds(pl.multiple_of(SIDE + 8 * c, 8), 8))

            planes_of(top + REACH, bottom - REACH, 0)
            for k in (2, 3):
                step_do(step - 1, source, k, "start")

            @pl.loop(1, groups)
            def _(c, planes_of=planes_of):
                planes_of(top + REACH, bottom - REACH, c)

            for k in (0, 1):
                step_do(step - 1, source, k, "wait_recv")

            @pl.loop(0, groups)
            def _(c, planes_of=planes_of):
                planes_of(top, top + REACH, c)
                planes_of(bottom - REACH, bottom, c)

            for k in (2, 3):
                step_do(step - 1, source, k, "wait_recv")

            def done(z, at, c, up, down, source=source, target=target, final=final):
                rate = speed[z, at, :]
                growth = jnp.sqrt(jnp.where(rate > 0.0, up, down))
                value = source[z, at, :] - (TIME_STEP / 6.0) * (rate * growth)
                if final:
                    next_ref[z - MARGIN, pl.ds(8 * c, 8), :] = value + 1.0
                    speed_ref[z - MARGIN, pl.ds(8 * c, 8), :] = rate
                else:
                    target[z, at, :] = value

            if final:
                plane_growth(source, gp, gm, top, bottom, done)
            else:
                plane_growth(source, gp, gm, top, top + edge, done)
                plane_growth(source, gp, gm, bottom - edge, bottom, done)
                step_do(step, target, 0, "start")
                plane_growth(source, gp, gm, top + edge, bottom - edge, done)
                step_do(step, target, 1, "start")
            for k in range(4):
                step_do(step - 1, source, k, "wait_send")
            source, target = target, source

    pl.run_scoped(scoped, pltpu.VMEM(phi.shape, f32), pltpu.VMEM(phi.shape, f32))


def per_device(displacement, material, level_set, wide, narrow):
    own_z, own_y, lanes = level_set.shape
    loads, comps, size_x, size_y, size_z = displacement.shape
    fields = loads * comps
    deep = own_z + 2 * MARGIN
    groups = own_y // 8
    tiles = size_z // 128
    padded = -(-(size_z + 2 * MARGIN) // 8) * 8
    result = jax.ShapeDtypeStruct((own_z, own_y, lanes), f32)
    dma = pltpu.SemaphoreType.DMA
    vmem = pl.BlockSpec(memory_space=pltpu.VMEM)
    hbm = pl.BlockSpec(memory_space=pl.ANY)
    return pl.pallas_call(
        functools.partial(kernel, wide=wide, narrow=narrow),
        out_shape=(result, result),
        in_specs=[hbm, vmem, hbm],
        out_specs=(vmem, vmem),
        scratch_shapes=[
            pltpu.VMEM((fields, size_x + 3, size_y + 8, size_z), f32),
            pltpu.VMEM((tiles, size_x * size_y, 128), f32),
            pltpu.VMEM((tiles, size_x * size_y, 128), f32),
            pltpu.VMEM((groups, padded, 128), f32),
            pltpu.VMEM((wide, groups + 2, -(-deep // 8) * 8, 128), f32),
            pltpu.VMEM((deep, own_y + 2 * SIDE, lanes), f32),
            pltpu.VMEM((deep, own_y + 2 * SIDE, lanes), f32),
            pltpu.VMEM((8, 128), f32),
            pltpu.VMEM((wide, 8, 128), f32),
            pltpu.VMEM((8, 128), f32),
            pltpu.VMEM((narrow, 8, 128), f32),
            dma((3,)), dma((2, 3, groups)), dma((2, 3, groups)), dma((2, 3)), dma((2, 3)), dma((4,)), dma((4,)),
            dma, dma((8,)), dma((8,)),
            dma((groups,)), dma((groups, wide)), dma((groups, wide)),
            dma((2, wide)), dma((2, wide)),
            dma((wide,)), dma((wide,)), dma((narrow,)), dma((narrow,)),
            dma((HJ_STEPS - 1, 4)), dma((HJ_STEPS - 1, 4)),
        ],
        compiler_params=pltpu.CompilerParams(
            vmem_limit_bytes=62 << 20, collective_id=0, has_side_effects=True
        ),
    )(
        displacement.reshape(fields, size_x, size_y, size_z),
        jnp.swapaxes(material, 1, 2),
        level_set,
    )


def solution(mesh):
    return jax.shard_map(
        functools.partial(per_device, wide=mesh.shape["wide"], narrow=mesh.shape["narrow"]),
        mesh=mesh,
        in_specs=(
            P(None, None, "wide", "narrow", None),
            P("wide", "narrow", None),
            P("wide", "narrow", None),
        ),
        out_specs=(P("wide", "narrow", None), P("wide", "narrow", None)),
        check_vma=False,
    )
```

```python
import functools

import jax
import jax.numpy as jnp
from jax import lax
from jax.experimental import pallas as pl
from jax.experimental.pallas import tpu as pltpu
from jax.sharding import PartitionSpec as P

BZ = 16
EXT_PASSES = 4
HJ_STEPS = 3
SHEAR = 0.384615
LAME = 0.576923
WENO_EPS = 1e-06
TIME_STEP = 0.3
TAP_SCALE = 1.0 / (48.0 * 48.0 * 8.0)
MARGIN = EXT_PASSES
SIDE = 8
REACH = 3
MESH = pl.DeviceIdType.MESH
f32 = jnp.float32


def val_taps(a, b, c, d):
    return (a + d) + 23.0 * (b + c)


def der_taps(a, b, c, d):
    return (d - a) + 5.0 * (c - b)


def z_filters(u):
    size = u.shape[-1]
    rows = u.shape[0]
    lane = lax.broadcasted_iota(jnp.int32, (rows, 128), 1)
    count = size // 128
    tiles = [u[:, t * 128:(t + 1) * 128] for t in range(count)]
    zero = jnp.zeros((rows, 128), f32)
    up = [pltpu.roll(t, 1, 1) for t in tiles]
    one = [pltpu.roll(t, 127, 1) for t in tiles] + [zero]
    two = [pltpu.roll(t, 126, 1) for t in tiles] + [zero]
    vals, ders = [], []
    for t in range(count):
        before = jnp.where(lane == 0, up[t - 1] if t else zero, up[t])
        after = jnp.where(lane == 127, one[t + 1], one[t])
        second = jnp.where(lane >= 126, two[t + 1], two[t])
        vals.append(val_taps(before, tiles[t], after, second))
        ders.append(der_taps(before, tiles[t], after, second))
    return vals, ders


def minus_side(e0, e1, t0, t1, c1, c3, p, q6, r3):
    low = p * (e0 + (c1 + c1)) + q6 * (e0 + t1) + r3 * (t1 + c3)
    return low, (p + q6) + r3


def plus_side(e0, e1, t0, t1, c1, c3, r, q6, p3):
    high = r * (e1 + (c3 + c3)) + q6 * (e1 + t0) + p3 * (t0 + c1)
    return high, (r + q6) + p3


EPS = 0.75 * WENO_EPS


def both_sides(d6, e0, e1, s0, s2, q0, q1, q2, g0, g1, t0, t1):
    c1 = e0 + s0
    c3 = e1 - s2
    a = q0 + g0 * c1
    b = q1 + g0 * e1
    c = q2 + g1 * c3
    a, b, c = a * a, b * b, c * c
    p, q6, r = b * c, 6.0 * (a * c), a * b
    low, low_sum = minus_side(e0, e1, t0, t1, c1, c3, p, q6, 3.0 * r)
    high, high_sum = plus_side(e0, e1, t0, t1, c1, c3, r, q6, 3.0 * p)
    return d6 + low / low_sum, high / high_sum - d6


def godunov(minus, plus):
    up = jnp.maximum(jnp.maximum(minus, plus), 0.0)
    down = jnp.minimum(jnp.minimum(minus, plus), 0.0)
    return up * up, down * down


def along_lanes(mid):
    size = mid.shape[-1]
    lane = lax.broadcasted_iota(jnp.int32, mid.shape, 1)
    u = []
    for k in range(-3, 4):
        if k == 0:
            u.append(mid)
            continue
        moved = pltpu.roll(mid, (-k) % size, 1)
        u.append(jnp.where(lane < -k if k < 0 else lane >= size - k, 0.0, moved))
    d = [u[k + 1] - u[k] for k in range(6)]
    e0, e1, e2, e3, e4 = [d[k + 1] - d[k] for k in range(5)]
    s = [e1 - e0, e2 - e1, e3 - e2, e4 - e3]
    q = [x * x + EPS for x in s]
    g = [0.75 * x for x in (e1, e2, e3)]
    t = [x + x for x in (e1, e2, e3)]
    c1, c3 = e1 + s[0], e2 - s[2]
    a, b, c = q[0] + g[0] * c1, q[1] + g[0] * e2, q[2] + g[1] * c3
    a, b, c = a * a, b * b, c * c
    low, low_sum = minus_side(e1, e2, t[0], t[1], c1, c3, b * c, 6.0 * (a * c), 3.0 * (a * b))
    c1, c3 = e2 + s[1], e3 - s[3]
    a, b, c = q[1] + g[1] * c1, q[2] + g[1] * e3, q[3] + g[2] * c3
    a, b, c = a * a, b * b, c * c
    high, high_sum = plus_side(e2, e3, t[1], t[2], c1, c3, a * b, 6.0 * (a * c), 3.0 * (b * c))
    return 6.0 * d[2] + low / low_sum, high / high_sum - 6.0 * d[3]


def along_rows(ref, z, start, count):
    u = [ref[z, pl.ds(start + k, count), :] for k in range(-2, 4)]
    d = [u[k + 1] - u[k] for k in range(5)]
    e = [d[k + 1] - d[k] for k in range(4)]
    s = [e[k + 1] - e[k] for k in range(3)]
    q = [x * x + EPS for x in s]
    return both_sides(
        6.0 * d[2], e[1], e[2], s[0], s[2], q[0], q[1], q[2], 0.75 * e[1], 0.75 * e[2], e[1] + e[1], e[2] + e[2]
    )


def along_planes(ref, gp, gm, z_lo, z_hi, at):
    u = [ref[z_lo - 3 + k, at, :] for k in range(5)]
    d = [u[k + 1] - u[k] for k in range(4)]
    e = [d[k + 1] - d[k] for k in range(3)]
    s = [e[k + 1] - e[k] for k in range(2)]
    q = [x * x + EPS for x in s]
    g = 0.75 * e[1]
    t = e[1] + e[1]
    newest, d_mid, d_new = u[4], d[2], d[3]
    behind = None
    for z in range(z_lo - 1, z_hi):
        plane = ref[z + 3, at, :]
        d_next = plane - newest
        e_next = d_next - d_new
        s_next = e_next - e[2]
        q_next = s_next * s_next + EPS
        g_next = 0.75 * e[2]
        t_next = e[2] + e[2]
        minus, plus = both_sides(
            6.0 * d_mid, e[1], e[2], s[0], s_next, q[0], q[1], q_next, g, g_next, t, t_next
        )
        if behind is not None:
            up, down = godunov(behind, plus)
            gp[z, at, :] = up
            gm[z, at, :] = down
        behind = minus
        newest, d_mid, d_new = plane, d_new, d_next
        e = [e[1], e[2], e_next]
        s = [s[1], s_next]
        q = [q[1], q_next]
        g, t = g_next, t_next


def block_flips(blocks):
    row = lax.broadcasted_iota(jnp.int32, (8, 128), 0)
    part = lax.broadcasted_iota(jnp.int32, (8, 128), 1) // 16
    far = [pltpu.roll(x, 4, 0) for x in blocks]
    far = [pltpu.roll(x, 64, 1) for x in far]
    same = (row // 4) % 2 == (part // 4) % 2
    blocks = [jnp.where(same, x, y) for x, y in zip(blocks, far)]
    for bit in (2, 1):
        row_bit, part_bit = (row // bit) % 2, (part // bit) % 2
        down = [pltpu.roll(x, bit, 0) for x in blocks]
        up = [pltpu.roll(x, 8 - bit, 0) for x in blocks]
        down = [pltpu.roll(x, 128 - 16 * bit, 1) for x in down]
        up = [pltpu.roll(x, 16 * bit, 1) for x in up]
        same, below = row_bit == part_bit, row_bit > part_bit
        blocks = [jnp.where(same, x, jnp.where(below, y, z)) for x, y, z in zip(blocks, down, up)]
    return blocks


def kernel(
    disp, mat, lev, next_ref, speed_ref,
    field, energy, stiff, packed, arrived, phi, psi, gp, gm, pull, keep, one, two, peak_out, peak_in, peak_mid, peak_all,
    own_sem, x_send, x_recv, y_send, y_recv, c_send, c_recv, lev_sem, lev_send, lev_recv,
    a_sem, a_send, a_recv, f_send, f_recv, p_send, p_recv, n_send, n_recv, e_send, e_recv,
    *, wide, narrow,
):
    i = lax.axis_index("wide")
    j = lax.axis_index("narrow")
    fields, size_x, size_y, size_z = disp.shape
    own_z, own_y, lanes = lev.shape
    deep, rows, _ = phi.shape
    tiles = size_z // 128
    groups = own_y // 8
    tail = size_y
    reach_y = REACH if lanes == 128 else SIDE
    slots = groups + 2
    has = {(-1, 0): i > 0, (1, 0): i < wide - 1, (0, -1): j > 0, (0, 1): j < narrow - 1}
    for a in (-1, 1):
        for b in (-1, 1):
            has[(a, b)] = has[(a, 0)] & has[(0, b)]
    around = [(-1, 0), (1, 0), (0, -1), (0, 1), (-1, -1), (-1, 1), (1, -1), (1, 1)]

    def remote(src, dst, send, recv, w, n):
        return pltpu.make_async_remote_copy(
            src_ref=src, dst_ref=dst, send_sem=send, recv_sem=recv,
            device_id={"wide": w, "narrow": n}, device_id_type=MESH,
        )

    own_copies = [
        pltpu.make_async_copy(
            disp.at[3 * l:3 * l + 3], field.at[3 * l:3 * l + 3, 0:size_x, 0:size_y], own_sem.at[l]
        )
        for l in range(3)
    ]
    lev_copy = pltpu.make_async_copy(
        lev, phi.at[MARGIN:MARGIN + own_z, SIDE:SIDE + own_y], lev_sem
    )

    def plane_part(dx):
        if dx < 0:
            return slice(0, 2), slice(size_x, size_x + 2)
        if dx > 0:
            return slice(size_x - 1, size_x), slice(size_x + 2, size_x + 3)
        return slice(0, size_x), slice(0, size_x)

    def row_part(dy):
        if dy < 0:
            return slice(0, 2), slice(tail, tail + 2)
        return slice(size_y - 1, size_y), slice(tail + 7, tail + 8)

    def x_copy(dx, l, b):
        src, dst = plane_part(dx)
        at = slice(8 * b, 8 * b + 8)
        k = (dx + 1) // 2
        return remote(
            disp.at[3 * l:3 * l + 3, src, at], field.at[3 * l:3 * l + 3, dst, at],
            x_send.at[k, l, b], x_recv.at[k, l, b], i + dx, j,
        )

    def y_copy(dy, l):
        src, dst = row_part(dy)
        k = (dy + 1) // 2
        return remote(
            disp.at[3 * l:3 * l + 3, :, src], field.at[3 * l:3 * l + 3, 0:size_x, dst],
            y_send.at[k, l], y_recv.at[k, l], i, j + dy,
        )

    def c_copy(dx, dy):
        xs, xd = plane_part(dx)
        ys, yd = row_part(dy)
        k = (dx + 1) + (dy + 1) // 2
        return remote(
            disp.at[:, xs, ys], field.at[:, xd, yd], c_send.at[k], c_recv.at[k], i + dx, j + dy
        )

    def lev_part(step, size, width, before):
        if step < 0:
            return slice(0, width), slice(before + size, before + size + width)
        if step > 0:
            return slice(size - width, size), slice(before - width, before)
        return slice(0, size), slice(before, before + size)

    def lev_send_copy(k):
        dx, dy = around[k]
        zs, zd = lev_part(dx, own_z, REACH, MARGIN)
        ys, yd = lev_part(dy, own_y, reach_y, SIDE)
        return remote(lev.at[zs, ys], phi.at[zd, yd], lev_send.at[k], lev_recv.at[k], i + dx, j + dy)

    def step_copy(n, ref, k):
        dx, dy = around[k]
        zs, zd = lev_part(dx, own_z, REACH, 0)
        ys, yd = lev_part(dy, own_y, reach_y, 0)

        def tile(z, y):
            return ref.at[slice(z.start + MARGIN, z.stop + MARGIN), slice(y.start + SIDE, y.stop + SIDE)]

        return remote(tile(zs, ys), tile(zd, yd), e_send.at[n, k], e_recv.at[n, k], i + dx, j + dy)

    def step_do(n, ref, k, what):
        dx, dy = around[k]
        sign = -1 if what == "wait_recv" else 1

        @pl.when(has[(sign * dx, sign * dy)])
        def _():
            getattr(step_copy(n, ref, k), what)()

    for copy in own_copies:
        copy.start()
    lev_copy.start()

    barrier = pltpu.get_barrier_semaphore()

    @pl.loop(1, wide)
    def _(k):
        pl.semaphore_signal(
            barrier, inc=1, device_id={"wide": (i + k) % wide, "narrow": j}, device_id_type=MESH
        )

    @pl.loop(1, narrow)
    def _(k):
        pl.semaphore_signal(
            barrier, inc=1, device_id={"wide": i, "narrow": (j + k) % narrow}, device_id_type=MESH
        )

    for dx, dy in around[4:]:
        @pl.when(has[(dx, dy)])
        def _(dx=dx, dy=dy):
            pl.semaphore_signal(
                barrier, inc=1, device_id={"wide": i + dx, "narrow": j + dy}, device_id_type=MESH
            )
    beside_x = jnp.where(i > 0, 1, 0) + jnp.where(i < wide - 1, 1, 0)
    beside_y = jnp.where(j > 0, 1, 0) + jnp.where(j < narrow - 1, 1, 0)
    pl.semaphore_wait(barrier, wide - 1 + narrow - 1 + beside_x * beside_y)

    for k in range(8):
        @pl.when(has[around[k]])
        def _(k=k):
            lev_send_copy(k).start()
    for dy in (-1, 1):
        @pl.when(has[(0, dy)])
        def _(dy=dy):
            for l in range(3):
                y_copy(dy, l).start()
    for b in (0,):
        for dx in (-1, 1):
            @pl.when(has[(dx, 0)])
            def _(dx=dx, b=b):
                for l in range(3):
                    x_copy(dx, l, b).start()
    for dx, dy in around[4:]:
        @pl.when(has[(dx, dy)])
        def _(dx=dx, dy=dy):
            c_copy(dx, dy).start()
    for b in (1,2,3,):
        for dx in (-1, 1):
            @pl.when(has[(dx, 0)])
            def _(dx=dx, b=b):
                for l in range(3):
                    x_copy(dx, l, b).start()

    for dx, planes in ((1, (size_x, size_x + 1)), (-1, (size_x + 2,))):
        @pl.when(jnp.logical_not(has[(dx, 0)]))
        def _(planes=planes):
            @pl.loop(0, fields)
            def _(f):
                for p in planes:
                    field[f, p] = jnp.zeros(field.shape[2:], f32)

    for dy, lo, hi in ((1, tail, tail + 2), (-1, tail + 7, tail + 8)):
        @pl.when(jnp.logical_not(has[(0, dy)]))
        def _(lo=lo, hi=hi):
            @pl.loop(0, fields)
            def _(f):
                for p in range(size_x + 3):
                    field[f, p, lo:hi, :] = jnp.zeros((hi - lo, size_z), f32)

    block = lax.broadcasted_iota(jnp.int32, (mat.shape[1], size_z), 0)
    column = lax.broadcasted_iota(jnp.int32, (mat.shape[1], size_z), 1) // BZ
    spread = jnp.where(block == column, 1.0, 0.0)

    @pl.loop(0, size_x // 4)
    def _(k):
        for p in range(4):
            solid = lax.dot_general(
                mat[4 * k + p].astype(f32), spread, (((0,), (0,)), ((), ())), preferred_element_type=f32
            )
            for t in range(tiles):
                at = pl.ds(pl.multiple_of((4 * k + p) * size_y, 8), size_y)
                stiff[t, at, :] = 0.2 + 0.8 * solid[:, t * 128:(t + 1) * 128]
                energy[t, at, :] = jnp.zeros((size_y, 128), f32)

    for b in range(groups):
        packed[b] = jnp.zeros(packed.shape[1:], f32)
    peak_out[...] = jnp.zeros(peak_out.shape, f32)

    @pl.loop(0, deep)
    def _(z):
        psi[z] = jnp.zeros(psi.shape[1:], f32)

    def inside(z, lo, shape):
        here = i * own_z - MARGIN + z
        row = lax.broadcasted_iota(jnp.int32, shape, 0) + (lo + j * own_y - SIDE)
        end = narrow * own_y
        lowest = jnp.where((here >= 0) & (here < wide * own_z), 0, end)
        return (row >= lowest) & (row < end)

    def most(count, options):
        return next(n for n in options if count % n == 0)

    flat = arrived.reshape(arrived.shape[0] * slots * arrived.shape[2], 128)
    stride = slots * arrived.shape[2]

    def unpack(slot):
        batch = most(deep, (8, 7, 6, 5, 4, 3, 2, 1))

        @pl.loop(0, deep // batch)
        def _(k):
            raw = []
            for r in range(batch):
                for h in range(wide // 8):
                    first = h * 8 * stride + slot * arrived.shape[2] + batch * k + r
                    raw.append(flat[pl.ds(first, 8, stride=stride), :])
            raw = block_flips(raw)
            for r in range(batch):
                pieces = [raw.pop(0) for _ in range(wide // 8)]
                held = pieces[0] if len(pieces) == 1 else jnp.concatenate(pieces, axis=1)
                one[batch * k + r, pl.ds(8 * slot, 8), :] = held

    def energy_phase(val, der):
        def filter_rows(f, p, at, spots):
            vals, ders = z_filters(field[f, p, at, :])
            for t in range(tiles):
                for spot in spots:
                    val[f, p, t, spot, :] = vals[t]
                    der[f, p, t, spot, :] = ders[t]

        tail_spots = (slice(0, 8), slice(8 + size_y, 16 + size_y))

        for l in range(3):
            own_copies[l].wait()

            @pl.loop(0, 3 * size_x // 2)
            def _(k, l=l):
                for p in range(2):
                    filter_rows(
                        3 * l + (2 * k) // size_x, (2 * k) % size_x + p, slice(0, size_y),
                        (slice(8, 8 + size_y),),
                    )

        for dy in (-1, 1):
            @pl.when(has[(0, -dy)])
            def _(dy=dy):
                for l in range(3):
                    y_copy(dy, l).wait_recv()

        @pl.loop(0, fields)
        def _(f):
            for p in range(size_x):
                filter_rows(f, p, slice(tail, tail + 8), tail_spots)

        def march_planes(f, t, y, planes, out):
            held = []
            for n, p in enumerate(planes):
                v = [[val[f + c, p, t, pl.ds(y + 7 + k, 8), :] for k in range(4)] for c in range(3)]
                w = [[der[f + c, p, t, pl.ds(y + 7 + k, 8), :] for k in range(4)] for c in range(3)]
                vv = [val_taps(*x) for x in v]
                vd = [der_taps(*x) for x in v]
                dv = [val_taps(*x) for x in w]
                held.append((vv[0], vd[0], dv[0], vv[1], vd[1], vv[2], dv[2], dv[1] + vd[2]))
                if len(held) < 4:
                    continue
                line = list(zip(*held))
                held = held[1:]
                exx = der_taps(*line[0])
                eyy = val_taps(*line[4])
                ezz = val_taps(*line[6])
                exy = val_taps(*line[1]) + der_taps(*line[3])
                exz = val_taps(*line[2]) + der_taps(*line[5])
                eyz = val_taps(*line[7])
                trace = exx + eyy + ezz
                square = (exx * exx + eyy * eyy + ezz * ezz) + 0.5 * (exy * exy + exz * exz + eyz * eyz)
                density = (SHEAR * TAP_SCALE * TAP_SCALE) * square
                density = density + (0.5 * LAME * TAP_SCALE * TAP_SCALE) * (trace * trace)
                at = pl.ds(out[n - 3] * size_y + y, 8)
                energy[t, at, :] = energy[t, at, :] + density

        @pl.loop(0, 3 * tiles * groups)
        def _(k):
            y = pl.multiple_of((k % groups) * 8, 8)
            march_planes(
                3 * (k // (tiles * groups)), (k // groups) % tiles, y,
                list(range(size_x)), list(range(1, size_x - 2)),
            )

        lev_copy.wait()
        for k in range(8):
            dx, dy = around[k]

            @pl.when(has[(-dx, -dy)])
            def _(k=k):
                lev_send_copy(k).wait_recv()

        @pl.loop(0, deep)
        def _(z):
            for lo in range(0, rows, 16):
                at = pl.ds(lo, 16)
                held = phi[z, at, :]
                mask = inside(z, lo, held.shape)
                weight = 1.0 / (1.0 + 4.0 * held * held)
                pull[z, at, :] = weight
                keep[z, at, :] = jnp.where(mask, (1.0 - weight) * (1.0 / 6.0), 0.0)
                phi[z, at, :] = jnp.where(mask, held - 1.0, 0.0)

        def growth_piece(n):
            begin, end = MARGIN + own_z * n // 3, MARGIN + own_z * (n + 1) // 3

            @pl.loop(0, groups)
            def _(c):
                along_planes(phi, gp, gm, begin, end, pl.ds(pl.multiple_of(SIDE + 8 * c, 8), 8))

            plane_growth(phi, gp, gm, begin, end, None)

        def take_halo(b):
            for dx in (-1, 1):
                @pl.when(has[(-dx, 0)])
                def _(dx=dx):
                    for l in range(3):
                        x_copy(dx, l, b).wait_recv()

            @pl.loop(0, fields)
            def _(f):
                for p in range(size_x, size_x + 3):
                    filter_rows(f, p, slice(8 * b, 8 * b + 8), (slice(8 * b + 8, 8 * b + 16),))

        def send_group(b):
            y = 8 * b

            @pl.loop(0, 3 * tiles)
            def _(k):
                march_planes(3 * (k // tiles), k % tiles, y, [size_x + 2, 0, 1, 2], [0])
                march_planes(
                    3 * (k // tiles), k % tiles, y,
                    [size_x - 3, size_x - 2, size_x - 1, size_x, size_x + 1], [size_x - 2, size_x - 1],
                )

            for t in range(tiles):
                parts = []
                for s in range(8):
                    at = pl.ds(y + s, size_x, stride=size_y)
                    parts.append(energy[t, at, :] * stiff[t, at, :])
                block = jnp.concatenate(parts, axis=0)
                top = jnp.max(block.reshape(block.shape[0] // 8, 8, 128), axis=0)
                peak_out[...] = jnp.maximum(peak_out[...], top)
                packed[b, MARGIN + 128 * t:MARGIN + 128 * (t + 1), :] = block.T

            pltpu.make_async_copy(
                packed.at[b, pl.ds(i * own_z, deep)], arrived.at[i, b + 1, pl.ds(0, deep)], a_sem.at[b]
            ).start()

            @pl.loop(1, wide)
            def _(k):
                w = (i + k) % wide
                remote(
                    packed.at[b, pl.ds(w * own_z, deep)], arrived.at[i, b + 1, pl.ds(0, deep)],
                    a_send.at[b, w], a_recv.at[b, i], w, j,
                ).start()

        for dx, dy in around[4:]:
            @pl.when(has[(-dx, -dy)])
            def _(dx=dx, dy=dy):
                c_copy(dx, dy).wait_recv()

        @pl.loop(0, fields)
        def _(f):
            for p in range(size_x, size_x + 3):
                filter_rows(f, p, slice(tail, tail + 8), tail_spots)

        take_halo(0)
        for b in range(groups):
            if b < groups - 1:
                take_halo(b + 1)
            send_group(b)
            if b < groups - 1:
                growth_piece(b)

        def wide_peak(k):
            w = (i + k) % wide
            return remote(peak_out, peak_in.at[i], p_send.at[w], p_recv.at[i], w, j)

        @pl.loop(1, wide)
        def _(k):
            wide_peak(k).start()

        def from_wide(k):
            s = (i + k) % wide
            return remote(peak_out, peak_in.at[s], p_send.at[s], p_recv.at[s], s, j)

        peak_mid[...] = peak_out[...]

        @pl.loop(1, wide)
        def _(k):
            from_wide(k).wait_recv()
            peak_mid[...] = jnp.maximum(peak_mid[...], peak_in[(i + k) % wide])

        def narrow_peak(k):
            n = (j + k) % narrow
            return remote(peak_mid, peak_all.at[j], n_send.at[n], n_recv.at[j], i, n)

        def from_narrow(k):
            s = (j + k) % narrow
            return remote(peak_mid, peak_all.at[s], n_send.at[s], n_recv.at[s], i, s)

        @pl.loop(1, narrow)
        def _(k):
            narrow_peak(k).start()


        passed = ((0, -1, slots - 1), (groups - 1, 1, 0))

        def forward(n, s):
            b, near, slot = passed[n]
            return remote(
                arrived.at[s, b + 1, pl.ds(0, deep)], arrived.at[s, slot, pl.ds(0, deep)],
                f_send.at[n, s], f_recv.at[n, s], i, j + near,
            )

        for b in range(groups):
            pltpu.make_async_copy(
                packed.at[b, pl.ds(i * own_z, deep)], arrived.at[i, b + 1, pl.ds(0, deep)], a_sem.at[b]
            ).wait()

            @pl.loop(0, wide)
            def _(k, b=b):
                s = (i + wide - k) % wide

                @pl.when(k > 0)
                def _():
                    remote(
                        packed.at[b, pl.ds(s * own_z, deep)], arrived.at[s, b + 1, pl.ds(0, deep)],
                        a_send.at[b, s], a_recv.at[b, s], s, j,
                    ).wait_recv()

                for n in range(2):
                    if passed[n][0] == b:
                        @pl.when(has[(0, passed[n][1])])
                        def _(n=n):
                            forward(n, s).start()

            unpack(b + 1)

        peak_all[j] = peak_mid[...]

        @pl.loop(1, narrow)
        def _(k):
            from_narrow(k).wait_recv()
            peak_all[j] = jnp.maximum(peak_all[j], peak_all[(j + k) % narrow])

        for n in range(2):
            @pl.when(has[(0, -passed[n][1])])
            def _(n=n):
                @pl.loop(0, wide)
                def _(s):
                    forward(n, s).wait_recv()

            unpack(passed[n][2])

        for n in range(2):
            @pl.when(has[(0, passed[n][1])])
            def _(n=n):
                @pl.loop(0, wide)
                def _(s):
                    forward(n, s).wait_send()

        for b in range(groups):
            @pl.loop(1, wide)
            def _(k, b=b):
                w = (i + k) % wide
                remote(
                    packed.at[b, pl.ds(w * own_z, deep)], arrived.at[i, b + 1, pl.ds(0, deep)],
                    a_send.at[b, w], a_recv.at[b, i], w, j,
                ).wait_send()

        @pl.loop(1, wide)
        def _(k):
            wide_peak(k).wait_send()

        @pl.loop(1, narrow)
        def _(k):
            narrow_peak(k).wait_send()

        for dy in (-1, 1):
            @pl.when(has[(0, dy)])
            def _(dy=dy):
                for l in range(3):
                    y_copy(dy, l).wait_send()
        for dx in (-1, 1):
            @pl.when(has[(dx, 0)])
            def _(dx=dx):
                for l in range(3):
                    for b in range(groups):
                        x_copy(dx, l, b).wait_send()
        for dx, dy in around[4:]:
            @pl.when(has[(dx, dy)])
            def _(dx=dx, dy=dy):
                c_copy(dx, dy).wait_send()
        for k in range(8):
            @pl.when(has[around[k]])
            def _(k=k):
                lev_send_copy(k).wait_send()

    def plane_growth(source, gp, gm, begin, end, done):
        if end <= begin:
            return
        row = lax.broadcasted_iota(jnp.int32, (8, lanes), 0)
        batch = most(end - begin, (3, 2, 1)) if end - begin < 8 else most(end - begin, (4, 3, 2, 1))

        def one_plane(z):
            before, _ = along_rows(source, z, SIDE - 4, 8)
            before = pltpu.roll(before, 5, 0)
            for c in range(groups):
                at = pl.ds(SIDE + 8 * c, 8)
                here, plus = along_rows(source, z, SIDE + 8 * c, 8)
                moved = pltpu.roll(here, 1, 0)
                up_y, down_y = godunov(jnp.where(row == 0, before, moved), plus)
                before = moved
                up_x, down_x = godunov(*along_lanes(source[z, at, :]))
                up = gp[z, at, :] + (up_y + up_x)
                down = gm[z, at, :] + (down_y + down_x)
                if done is None:
                    gp[z, at, :] = jnp.sqrt(up)
                    gm[z, at, :] = jnp.sqrt(down)
                else:
                    done(z, at, c, up, down)

        @pl.loop(0, (end - begin) // batch)
        def _(k):
            for r in range(batch):
                one_plane(begin + batch * k + r)


    def march_phase():
        scale = jnp.max(peak_all[j]) + 1e-06

        @pl.loop(0, deep)
        def _(z):
            for lo in range(0, rows, 16):
                at = pl.ds(lo, 16)
                held = one[z, at, :]
                velocity = jnp.where(inside(z, lo, held.shape), held / scale - 0.5, 0.0)
                one[z, at, :] = velocity
                pull[z, at, :] = pull[z, at, :] * velocity

        top, bottom = MARGIN, MARGIN + own_z
        edge = 6
        source, target = one, two
        lane = lax.broadcasted_iota(jnp.int32, (8, lanes), 1)
        for step in range(EXT_PASSES):
            last = step == EXT_PASSES - 1
            lo, chunks = (SIDE, groups) if last else (SIDE - 4, groups + 1)

            def extend(planes, source=source, target=target, lo=lo, chunks=chunks, last=last):
                spots = [(z, lo + 8 * c) for z in planes for c in range(chunks)]
                mids = [source[z, pl.ds(start, 8), :] for z, start in spots]
                lows = [pltpu.roll(mid, 1, 1) for mid in mids]
                highs = [pltpu.roll(mid, lanes - 1, 1) for mid in mids]
                for (z, start), low, high in zip(spots, lows, highs):
                    at = pl.ds(start, 8)
                    total = source[z - 1, at, :] + source[z + 1, at, :]
                    total = total + (source[z, pl.ds(start - 1, 8), :] + source[z, pl.ds(start + 1, 8), :])
                    low = jnp.where(lane == 0, 0.0, low)
                    high = jnp.where(lane == lanes - 1, 0.0, high)
                    value = pull[z, at, :] + keep[z, at, :] * (total + (low + high))
                    target[z, at, :] = value
                    if last:
                        growth = jnp.where(value > 0.0, gp[z, at, :], gm[z, at, :])
                        psi[z, at, :] = phi[z, at, :] - (TIME_STEP / 6.0) * (value * growth)

            def extend_all(begin, end, extend=extend):
                if end <= begin:
                    return
                size = most(end - begin, (6, 5, 4, 3, 2, 1))

                @pl.loop(0, (end - begin) // size)
                def _(k):
                    extend([begin + size * k + r for r in range(size)])

            if last:
                extend_all(top, top + edge)
                extend_all(bottom - edge, bottom)
                step_do(0, psi, 0, "start")
                extend_all(top + edge, bottom - edge)
                step_do(0, psi, 1, "start")
            else:
                extend_all(step + 1, deep - step - 1)
            source, target = target, source
        speed = source

        source, target = psi, phi
        for step in range(1, HJ_STEPS):
            final = step == HJ_STEPS - 1

            def planes_of(begin, end, c, source=source):
                along_planes(source, gp, gm, begin, end, pl.ds(pl.multiple_of(SIDE + 8 * c, 8), 8))

            planes_of(top + REACH, bottom - REACH, 0)
            for k in (2, 3):
                step_do(step - 1, source, k, "start")

            @pl.loop(1, groups)
            def _(c, planes_of=planes_of):
                planes_of(top + REACH, bottom - REACH, c)

            for k in (0, 1):
                step_do(step - 1, source, k, "wait_recv")

            @pl.loop(0, groups)
            def _(c, planes_of=planes_of):
                planes_of(top, top + REACH, c)
                planes_of(bottom - REACH, bottom, c)

            for k in (2, 3):
                step_do(step - 1, source, k, "wait_recv")

            def done(z, at, c, up, down, source=source, target=target, final=final):
                rate = speed[z, at, :]
                growth = jnp.sqrt(jnp.where(rate > 0.0, up, down))
                value = source[z, at, :] - (TIME_STEP / 6.0) * (rate * growth)
                if final:
                    next_ref[z - MARGIN, pl.ds(8 * c, 8), :] = value
                    speed_ref[z - MARGIN, pl.ds(8 * c, 8), :] = rate
                else:
                    target[z, at, :] = value

            if final:
                plane_growth(source, gp, gm, top, bottom, done)
            else:
                plane_growth(source, gp, gm, top, top + edge, done)
                plane_growth(source, gp, gm, bottom - edge, bottom, done)
                step_do(step, target, 0, "start")
                plane_growth(source, gp, gm, top + edge, bottom - edge, done)
                step_do(step, target, 1, "start")
            for k in range(4):
                step_do(step - 1, source, k, "wait_send")
            source, target = target, source

    pl.run_scoped(
        energy_phase,
        pltpu.VMEM((fields, size_x + 3, tiles, size_y + 16, 128), f32),
        pltpu.VMEM((fields, size_x + 3, tiles, size_y + 16, 128), f32),
    )
    march_phase()


def per_device(displacement, material, level_set, wide, narrow):
    own_z, own_y, lanes = level_set.shape
    loads, comps, size_x, size_y, size_z = displacement.shape
    fields = loads * comps
    deep = own_z + 2 * MARGIN
    groups = own_y // 8
    tiles = size_z // 128
    padded = -(-(size_z + 2 * MARGIN) // 8) * 8
    result = jax.ShapeDtypeStruct((own_z, own_y, lanes), f32)
    dma = pltpu.SemaphoreType.DMA
    vmem = pl.BlockSpec(memory_space=pltpu.VMEM)
    hbm = pl.BlockSpec(memory_space=pl.ANY)
    level, speed = pl.pallas_call(
        functools.partial(kernel, wide=wide, narrow=narrow),
        out_shape=(result, result),
        in_specs=[hbm, vmem, hbm],
        out_specs=(vmem, vmem),
        scratch_shapes=[
            pltpu.VMEM((fields, size_x + 3, size_y + 8, size_z), f32),
            pltpu.VMEM((tiles, size_x * size_y, 128), f32),
            pltpu.VMEM((tiles, size_x * size_y, 128), f32),
            pltpu.VMEM((groups, padded, 128), f32),
            pltpu.VMEM((wide, groups + 2, -(-deep // 8) * 8, 128), f32),
            *[pltpu.VMEM((deep, own_y + 2 * SIDE, lanes), f32)] * 8,
            pltpu.VMEM((8, 128), f32),
            pltpu.VMEM((wide, 8, 128), f32),
            pltpu.VMEM((8, 128), f32),
            pltpu.VMEM((narrow, 8, 128), f32),
            dma((3,)), dma((2, 3, groups)), dma((2, 3, groups)), dma((2, 3)), dma((2, 3)), dma((4,)), dma((4,)),
            dma, dma((8,)), dma((8,)),
            dma((groups,)), dma((groups, wide)), dma((groups, wide)),
            dma((2, wide)), dma((2, wide)),
            dma((wide,)), dma((wide,)), dma((narrow,)), dma((narrow,)),
            dma((HJ_STEPS - 1, 4)), dma((HJ_STEPS - 1, 4)),
        ],
        compiler_params=pltpu.CompilerParams(
            vmem_limit_bytes=62 << 20, collective_id=0, has_side_effects=True
        ),
    )(
        displacement.reshape(fields, size_x, size_y, size_z),
        jnp.swapaxes(material, 1, 2),
        level_set,
    )

    def finish(level_in, speed_in, level_out, speed_out):
        level_out[...] = level_in[...] + 1.0
        speed_out[...] = speed_in[...]

    return pl.pallas_call(
        finish,
        out_shape=(result, result),
        in_specs=[vmem, vmem],
        out_specs=(vmem, vmem),
    )(level, speed)


def solution(mesh):
    return jax.shard_map(
        functools.partial(per_device, wide=mesh.shape["wide"], narrow=mesh.shape["narrow"]),
        mesh=mesh,
        in_specs=(
            P(None, None, "wide", "narrow", None),
            P("wide", "narrow", None),
            P("wide", "narrow", None),
        ),
        out_specs=(P("wide", "narrow", None), P("wide", "narrow", None)),
        check_vma=False,
    )
```

```python
import functools

import jax
import jax.numpy as jnp
from jax import lax
from jax.experimental import pallas as pl
from jax.experimental.pallas import tpu as pltpu
from jax.sharding import PartitionSpec as P

BZ = 16
EXT_PASSES = 4
HJ_STEPS = 3
SHEAR = 0.384615
LAME = 0.576923
WENO_EPS = 1e-06
TIME_STEP = 0.3
TAP_SCALE = 1.0 / (48.0 * 48.0 * 8.0)
MARGIN = EXT_PASSES
SIDE = 8
REACH = 3
MESH = pl.DeviceIdType.MESH
f32 = jnp.float32


def val_taps(a, b, c, d):
    return (a + d) + 23.0 * (b + c)


def der_taps(a, b, c, d):
    return (d - a) + 5.0 * (c - b)


def z_filters(u):
    size = u.shape[-1]
    rows = u.shape[0]
    lane = lax.broadcasted_iota(jnp.int32, (rows, 128), 1)
    count = size // 128
    tiles = [u[:, t * 128:(t + 1) * 128] for t in range(count)]
    zero = jnp.zeros((rows, 128), f32)
    up = [pltpu.roll(t, 1, 1) for t in tiles]
    one = [pltpu.roll(t, 127, 1) for t in tiles] + [zero]
    two = [pltpu.roll(t, 126, 1) for t in tiles] + [zero]
    vals, ders = [], []
    for t in range(count):
        before = jnp.where(lane == 0, up[t - 1] if t else zero, up[t])
        after = jnp.where(lane == 127, one[t + 1], one[t])
        second = jnp.where(lane >= 126, two[t + 1], two[t])
        vals.append(val_taps(before, tiles[t], after, second))
        ders.append(der_taps(before, tiles[t], after, second))
    return vals, ders


def minus_side(e0, e1, t0, t1, c1, c3, p, q6, r3):
    low = p * (e0 + (c1 + c1)) + q6 * (e0 + t1) + r3 * (t1 + c3)
    return low, (p + q6) + r3


def plus_side(e0, e1, t0, t1, c1, c3, r, q6, p3):
    high = r * (e1 + (c3 + c3)) + q6 * (e1 + t0) + p3 * (t0 + c1)
    return high, (r + q6) + p3


EPS = 0.75 * WENO_EPS


def both_sides(d6, e0, e1, s0, s2, q0, q1, q2, g0, g1, t0, t1):
    c1 = e0 + s0
    c3 = e1 - s2
    a = q0 + g0 * c1
    b = q1 + g0 * e1
    c = q2 + g1 * c3
    a, b, c = a * a, b * b, c * c
    p, q6, r = b * c, 6.0 * (a * c), a * b
    low, low_sum = minus_side(e0, e1, t0, t1, c1, c3, p, q6, 3.0 * r)
    high, high_sum = plus_side(e0, e1, t0, t1, c1, c3, r, q6, 3.0 * p)
    return d6 + low / low_sum, high / high_sum - d6


def godunov(minus, plus):
    up = jnp.maximum(jnp.maximum(minus, plus), 0.0)
    down = jnp.minimum(jnp.minimum(minus, plus), 0.0)
    return up * up, down * down


def along_lanes(mid):
    size = mid.shape[-1]
    lane = lax.broadcasted_iota(jnp.int32, mid.shape, 1)
    u = []
    for k in range(-3, 4):
        if k == 0:
            u.append(mid)
            continue
        moved = pltpu.roll(mid, (-k) % size, 1)
        u.append(jnp.where(lane < -k if k < 0 else lane >= size - k, 0.0, moved))
    d = [u[k + 1] - u[k] for k in range(6)]
    e0, e1, e2, e3, e4 = [d[k + 1] - d[k] for k in range(5)]
    s = [e1 - e0, e2 - e1, e3 - e2, e4 - e3]
    q = [x * x + EPS for x in s]
    g = [0.75 * x for x in (e1, e2, e3)]
    t = [x + x for x in (e1, e2, e3)]
    c1, c3 = e1 + s[0], e2 - s[2]
    a, b, c = q[0] + g[0] * c1, q[1] + g[0] * e2, q[2] + g[1] * c3
    a, b, c = a * a, b * b, c * c
    low, low_sum = minus_side(e1, e2, t[0], t[1], c1, c3, b * c, 6.0 * (a * c), 3.0 * (a * b))
    c1, c3 = e2 + s[1], e3 - s[3]
    a, b, c = q[1] + g[1] * c1, q[2] + g[1] * e3, q[3] + g[2] * c3
    a, b, c = a * a, b * b, c * c
    high, high_sum = plus_side(e2, e3, t[1], t[2], c1, c3, a * b, 6.0 * (a * c), 3.0 * (b * c))
    return 6.0 * d[2] + low / low_sum, high / high_sum - 6.0 * d[3]


def along_rows(ref, z, start, count):
    u = [ref[z, pl.ds(start + k, count), :] for k in range(-2, 4)]
    d = [u[k + 1] - u[k] for k in range(5)]
    e = [d[k + 1] - d[k] for k in range(4)]
    s = [e[k + 1] - e[k] for k in range(3)]
    q = [x * x + EPS for x in s]
    return both_sides(
        6.0 * d[2], e[1], e[2], s[0], s[2], q[0], q[1], q[2], 0.75 * e[1], 0.75 * e[2], e[1] + e[1], e[2] + e[2]
    )


def along_planes(ref, gp, gm, z_lo, z_hi, at):
    u = [ref[z_lo - 3 + k, at, :] for k in range(5)]
    d = [u[k + 1] - u[k] for k in range(4)]
    e = [d[k + 1] - d[k] for k in range(3)]
    s = [e[k + 1] - e[k] for k in range(2)]
    q = [x * x + EPS for x in s]
    g = 0.75 * e[1]
    t = e[1] + e[1]
    newest, d_mid, d_new = u[4], d[2], d[3]
    behind = None
    for z in range(z_lo - 1, z_hi):
        plane = ref[z + 3, at, :]
        d_next = plane - newest
        e_next = d_next - d_new
        s_next = e_next - e[2]
        q_next = s_next * s_next + EPS
        g_next = 0.75 * e[2]
        t_next = e[2] + e[2]
        minus, plus = both_sides(
            6.0 * d_mid, e[1], e[2], s[0], s_next, q[0], q[1], q_next, g, g_next, t, t_next
        )
        if behind is not None:
            up, down = godunov(behind, plus)
            gp[z, at, :] = up
            gm[z, at, :] = down
        behind = minus
        newest, d_mid, d_new = plane, d_new, d_next
        e = [e[1], e[2], e_next]
        s = [s[1], s_next]
        q = [q[1], q_next]
        g, t = g_next, t_next


def block_flips(blocks):
    row = lax.broadcasted_iota(jnp.int32, (8, 128), 0)
    part = lax.broadcasted_iota(jnp.int32, (8, 128), 1) // 16
    far = [pltpu.roll(x, 4, 0) for x in blocks]
    far = [pltpu.roll(x, 64, 1) for x in far]
    same = (row // 4) % 2 == (part // 4) % 2
    blocks = [jnp.where(same, x, y) for x, y in zip(blocks, far)]
    for bit in (2, 1):
        row_bit, part_bit = (row // bit) % 2, (part // bit) % 2
        down = [pltpu.roll(x, bit, 0) for x in blocks]
        up = [pltpu.roll(x, 8 - bit, 0) for x in blocks]
        down = [pltpu.roll(x, 128 - 16 * bit, 1) for x in down]
        up = [pltpu.roll(x, 16 * bit, 1) for x in up]
        same, below = row_bit == part_bit, row_bit > part_bit
        blocks = [jnp.where(same, x, jnp.where(below, y, z)) for x, y, z in zip(blocks, down, up)]
    return blocks


def kernel(
    disp, mat, lev, next_ref, speed_ref,
    field, energy, stiff, packed, arrived, phi, psi, gp, gm, pull, keep, one, two, peak_out, peak_in, peak_mid, peak_all,
    own_sem, x_send, x_recv, y_send, y_recv, c_send, c_recv, lev_sem, lev_send, lev_recv,
    a_sem, a_send, a_recv, f_send, f_recv, p_send, p_recv, n_send, n_recv, e_send, e_recv,
    *, wide, narrow,
):
    i = lax.axis_index("wide")
    j = lax.axis_index("narrow")
    fields, size_x, size_y, size_z = disp.shape
    own_z, own_y, lanes = lev.shape
    deep, rows, _ = phi.shape
    tiles = size_z // 128
    groups = own_y // 8
    tail = size_y
    reach_y = REACH if lanes == 128 else SIDE
    slots = groups + 2
    has = {(-1, 0): i > 0, (1, 0): i < wide - 1, (0, -1): j > 0, (0, 1): j < narrow - 1}
    for a in (-1, 1):
        for b in (-1, 1):
            has[(a, b)] = has[(a, 0)] & has[(0, b)]
    around = [(-1, 0), (1, 0), (0, -1), (0, 1), (-1, -1), (-1, 1), (1, -1), (1, 1)]

    def remote(src, dst, send, recv, w, n):
        return pltpu.make_async_remote_copy(
            src_ref=src, dst_ref=dst, send_sem=send, recv_sem=recv,
            device_id={"wide": w, "narrow": n}, device_id_type=MESH,
        )

    own_copies = [
        pltpu.make_async_copy(
            disp.at[3 * l:3 * l + 3], field.at[3 * l:3 * l + 3, 0:size_x, 0:size_y], own_sem.at[l]
        )
        for l in range(3)
    ]
    lev_copy = pltpu.make_async_copy(
        lev, phi.at[MARGIN:MARGIN + own_z, SIDE:SIDE + own_y], lev_sem
    )

    def plane_part(dx):
        if dx < 0:
            return slice(0, 2), slice(size_x, size_x + 2)
        if dx > 0:
            return slice(size_x - 1, size_x), slice(size_x + 2, size_x + 3)
        return slice(0, size_x), slice(0, size_x)

    def row_part(dy):
        if dy < 0:
            return slice(0, 2), slice(tail, tail + 2)
        return slice(size_y - 1, size_y), slice(tail + 7, tail + 8)

    def x_copy(dx, l, b):
        src, dst = plane_part(dx)
        at = slice(8 * b, 8 * b + 8)
        k = (dx + 1) // 2
        return remote(
            disp.at[3 * l:3 * l + 3, src, at], field.at[3 * l:3 * l + 3, dst, at],
            x_send.at[k, l, b], x_recv.at[k, l, b], i + dx, j,
        )

    def y_copy(dy, l):
        src, dst = row_part(dy)
        k = (dy + 1) // 2
        return remote(
            disp.at[3 * l:3 * l + 3, :, src], field.at[3 * l:3 * l + 3, 0:size_x, dst],
            y_send.at[k, l], y_recv.at[k, l], i, j + dy,
        )

    def c_copy(dx, dy):
        xs, xd = plane_part(dx)
        ys, yd = row_part(dy)
        k = (dx + 1) + (dy + 1) // 2
        return remote(
            disp.at[:, xs, ys], field.at[:, xd, yd], c_send.at[k], c_recv.at[k], i + dx, j + dy
        )

    def lev_part(step, size, width, before):
        if step < 0:
            return slice(0, width), slice(before + size, before + size + width)
        if step > 0:
            return slice(size - width, size), slice(before - width, before)
        return slice(0, size), slice(before, before + size)

    def lev_send_copy(k):
        dx, dy = around[k]
        zs, zd = lev_part(dx, own_z, REACH, MARGIN)
        ys, yd = lev_part(dy, own_y, reach_y, SIDE)
        return remote(lev.at[zs, ys], phi.at[zd, yd], lev_send.at[k], lev_recv.at[k], i + dx, j + dy)

    def step_copy(n, ref, k):
        dx, dy = around[k]
        zs, zd = lev_part(dx, own_z, REACH, 0)
        ys, yd = lev_part(dy, own_y, reach_y, 0)

        def tile(z, y):
            return ref.at[slice(z.start + MARGIN, z.stop + MARGIN), slice(y.start + SIDE, y.stop + SIDE)]

        return remote(tile(zs, ys), tile(zd, yd), e_send.at[n, k], e_recv.at[n, k], i + dx, j + dy)

    def step_do(n, ref, k, what):
        dx, dy = around[k]
        sign = -1 if what == "wait_recv" else 1

        @pl.when(has[(sign * dx, sign * dy)])
        def _():
            getattr(step_copy(n, ref, k), what)()

    for copy in own_copies:
        copy.start()
    lev_copy.start()

    barrier = pltpu.get_barrier_semaphore()

    @pl.loop(1, wide)
    def _(k):
        pl.semaphore_signal(
            barrier, inc=1, device_id={"wide": (i + k) % wide, "narrow": j}, device_id_type=MESH
        )

    @pl.loop(1, narrow)
    def _(k):
        pl.semaphore_signal(
            barrier, inc=1, device_id={"wide": i, "narrow": (j + k) % narrow}, device_id_type=MESH
        )

    for dx, dy in around[4:]:
        @pl.when(has[(dx, dy)])
        def _(dx=dx, dy=dy):
            pl.semaphore_signal(
                barrier, inc=1, device_id={"wide": i + dx, "narrow": j + dy}, device_id_type=MESH
            )
    beside_x = jnp.where(i > 0, 1, 0) + jnp.where(i < wide - 1, 1, 0)
    beside_y = jnp.where(j > 0, 1, 0) + jnp.where(j < narrow - 1, 1, 0)
    pl.semaphore_wait(barrier, wide - 1 + narrow - 1 + beside_x * beside_y)

    for k in range(8):
        @pl.when(has[around[k]])
        def _(k=k):
            lev_send_copy(k).start()
    for dy in (-1, 1):
        @pl.when(has[(0, dy)])
        def _(dy=dy):
            for l in range(3):
                y_copy(dy, l).start()
    for b in (0,):
        for dx in (-1, 1):
            @pl.when(has[(dx, 0)])
            def _(dx=dx, b=b):
                for l in range(3):
                    x_copy(dx, l, b).start()
    for dx, dy in around[4:]:
        @pl.when(has[(dx, dy)])
        def _(dx=dx, dy=dy):
            c_copy(dx, dy).start()
    for b in (1,2,3,):
        for dx in (-1, 1):
            @pl.when(has[(dx, 0)])
            def _(dx=dx, b=b):
                for l in range(3):
                    x_copy(dx, l, b).start()

    for dx, planes in ((1, (size_x, size_x + 1)), (-1, (size_x + 2,))):
        @pl.when(jnp.logical_not(has[(dx, 0)]))
        def _(planes=planes):
            @pl.loop(0, fields)
            def _(f):
                for p in planes:
                    field[f, p] = jnp.zeros(field.shape[2:], f32)

    for dy, lo, hi in ((1, tail, tail + 2), (-1, tail + 7, tail + 8)):
        @pl.when(jnp.logical_not(has[(0, dy)]))
        def _(lo=lo, hi=hi):
            @pl.loop(0, fields)
            def _(f):
                for p in range(size_x + 3):
                    field[f, p, lo:hi, :] = jnp.zeros((hi - lo, size_z), f32)

    block = lax.broadcasted_iota(jnp.int32, (mat.shape[1], size_z), 0)
    column = lax.broadcasted_iota(jnp.int32, (mat.shape[1], size_z), 1) // BZ
    spread = jnp.where(block == column, 1.0, 0.0)

    @pl.loop(0, size_x // 4)
    def _(k):
        for p in range(4):
            solid = lax.dot_general(
                mat[4 * k + p].astype(f32), spread, (((0,), (0,)), ((), ())), preferred_element_type=f32
            )
            for t in range(tiles):
                at = pl.ds(pl.multiple_of((4 * k + p) * size_y, 8), size_y)
                stiff[t, at, :] = 0.2 + 0.8 * solid[:, t * 128:(t + 1) * 128]
                energy[t, at, :] = jnp.zeros((size_y, 128), f32)

    for b in range(groups):
        packed[b] = jnp.zeros(packed.shape[1:], f32)
    peak_out[...] = jnp.zeros(peak_out.shape, f32)

    @pl.loop(0, deep)
    def _(z):
        psi[z] = jnp.zeros(psi.shape[1:], f32)

    def inside(z, lo, shape):
        here = i * own_z - MARGIN + z
        row = lax.broadcasted_iota(jnp.int32, shape, 0) + (lo + j * own_y - SIDE)
        end = narrow * own_y
        lowest = jnp.where((here >= 0) & (here < wide * own_z), 0, end)
        return (row >= lowest) & (row < end)

    def most(count, options):
        return next(n for n in options if count % n == 0)

    flat = arrived.reshape(arrived.shape[0] * slots * arrived.shape[2], 128)
    stride = slots * arrived.shape[2]

    def unpack(slot):
        batch = most(deep, (8, 7, 6, 5, 4, 3, 2, 1))

        @pl.loop(0, deep // batch)
        def _(k):
            raw = []
            for r in range(batch):
                for h in range(wide // 8):
                    first = h * 8 * stride + slot * arrived.shape[2] + batch * k + r
                    raw.append(flat[pl.ds(first, 8, stride=stride), :])
            raw = block_flips(raw)
            for r in range(batch):
                pieces = [raw.pop(0) for _ in range(wide // 8)]
                held = pieces[0] if len(pieces) == 1 else jnp.concatenate(pieces, axis=1)
                one[batch * k + r, pl.ds(8 * slot, 8), :] = held

    def energy_phase(val, der):
        def filter_rows(f, p, at, spots):
            vals, ders = z_filters(field[f, p, at, :])
            for t in range(tiles):
                for spot in spots:
                    val[f, p, t, spot, :] = vals[t]
                    der[f, p, t, spot, :] = ders[t]

        tail_spots = (slice(0, 8), slice(8 + size_y, 16 + size_y))

        for l in range(3):
            own_copies[l].wait()

            @pl.loop(0, 3 * size_x // 2)
            def _(k, l=l):
                for p in range(2):
                    filter_rows(
                        3 * l + (2 * k) // size_x, (2 * k) % size_x + p, slice(0, size_y),
                        (slice(8, 8 + size_y),),
                    )

        for dy in (-1, 1):
            @pl.when(has[(0, -dy)])
            def _(dy=dy):
                for l in range(3):
                    y_copy(dy, l).wait_recv()

        @pl.loop(0, fields)
        def _(f):
            for p in range(size_x):
                filter_rows(f, p, slice(tail, tail + 8), tail_spots)

        def march_planes(f, t, y, planes, out):
            held = []
            for n, p in enumerate(planes):
                v = [[val[f + c, p, t, pl.ds(y + 7 + k, 8), :] for k in range(4)] for c in range(3)]
                w = [[der[f + c, p, t, pl.ds(y + 7 + k, 8), :] for k in range(4)] for c in range(3)]
                vv = [val_taps(*x) for x in v]
                vd = [der_taps(*x) for x in v]
                dv = [val_taps(*x) for x in w]
                held.append((vv[0], vd[0], dv[0], vv[1], vd[1], vv[2], dv[2], dv[1] + vd[2]))
                if len(held) < 4:
                    continue
                line = list(zip(*held))
                held = held[1:]
                exx = der_taps(*line[0])
                eyy = val_taps(*line[4])
                ezz = val_taps(*line[6])
                exy = val_taps(*line[1]) + der_taps(*line[3])
                exz = val_taps(*line[2]) + der_taps(*line[5])
                eyz = val_taps(*line[7])
                trace = exx + eyy + ezz
                square = (exx * exx + eyy * eyy + ezz * ezz) + 0.5 * (exy * exy + exz * exz + eyz * eyz)
                density = (SHEAR * TAP_SCALE * TAP_SCALE) * square
                density = density + (0.5 * LAME * TAP_SCALE * TAP_SCALE) * (trace * trace)
                at = pl.ds(out[n - 3] * size_y + y, 8)
                energy[t, at, :] = energy[t, at, :] + density

        @pl.loop(0, 3 * tiles * groups)
        def _(k):
            y = pl.multiple_of((k % groups) * 8, 8)
            march_planes(
                3 * (k // (tiles * groups)), (k // groups) % tiles, y,
                list(range(size_x)), list(range(1, size_x - 2)),
            )

        lev_copy.wait()
        for k in range(8):
            dx, dy = around[k]

            @pl.when(has[(-dx, -dy)])
            def _(k=k):
                lev_send_copy(k).wait_recv()

        @pl.loop(0, deep)
        def _(z):
            for lo in range(0, rows, 16):
                at = pl.ds(lo, 16)
                held = phi[z, at, :]
                mask = inside(z, lo, held.shape)
                weight = 1.0 / (1.0 + 4.0 * held * held)
                pull[z, at, :] = weight
                keep[z, at, :] = jnp.where(mask, (1.0 - weight) * (1.0 / 6.0), 0.0)
                phi[z, at, :] = jnp.where(mask, held - 1.0, 0.0)

        def growth_piece(n):
            begin, end = MARGIN + own_z * n // 3, MARGIN + own_z * (n + 1) // 3

            @pl.loop(0, groups)
            def _(c):
                along_planes(phi, gp, gm, begin, end, pl.ds(pl.multiple_of(SIDE + 8 * c, 8), 8))

            plane_growth(phi, gp, gm, begin, end, None)

        def take_halo(b):
            for dx in (-1, 1):
                @pl.when(has[(-dx, 0)])
                def _(dx=dx):
                    for l in range(3):
                        x_copy(dx, l, b).wait_recv()

            @pl.loop(0, fields)
            def _(f):
                for p in range(size_x, size_x + 3):
                    filter_rows(f, p, slice(8 * b, 8 * b + 8), (slice(8 * b + 8, 8 * b + 16),))

        def send_group(b):
            y = 8 * b

            @pl.loop(0, 3 * tiles)
            def _(k):
                march_planes(3 * (k // tiles), k % tiles, y, [size_x + 2, 0, 1, 2], [0])
                march_planes(
                    3 * (k // tiles), k % tiles, y,
                    [size_x - 3, size_x - 2, size_x - 1, size_x, size_x + 1], [size_x - 2, size_x - 1],
                )

            for t in range(tiles):
                parts = []
                for s in range(8):
                    at = pl.ds(y + s, size_x, stride=size_y)
                    parts.append(energy[t, at, :] * stiff[t, at, :])
                block = jnp.concatenate(parts, axis=0)
                top = jnp.max(block.reshape(block.shape[0] // 8, 8, 128), axis=0)
                peak_out[...] = jnp.maximum(peak_out[...], top)
                packed[b, MARGIN + 128 * t:MARGIN + 128 * (t + 1), :] = block.T

            pltpu.make_async_copy(
                packed.at[b, pl.ds(i * own_z, deep)], arrived.at[i, b + 1, pl.ds(0, deep)], a_sem.at[b]
            ).start()

            @pl.loop(1, wide)
            def _(k):
                w = (i + k) % wide
                remote(
                    packed.at[b, pl.ds(w * own_z, deep)], arrived.at[i, b + 1, pl.ds(0, deep)],
                    a_send.at[b, w], a_recv.at[b, i], w, j,
                ).start()

        for dx, dy in around[4:]:
            @pl.when(has[(-dx, -dy)])
            def _(dx=dx, dy=dy):
                c_copy(dx, dy).wait_recv()

        @pl.loop(0, fields)
        def _(f):
            for p in range(size_x, size_x + 3):
                filter_rows(f, p, slice(tail, tail + 8), tail_spots)

        take_halo(0)
        for b in range(groups):
            if b < groups - 1:
                take_halo(b + 1)
            send_group(b)
            if b < groups - 1:
                growth_piece(b)

        def wide_peak(k):
            w = (i + k) % wide
            return remote(peak_out, peak_in.at[i], p_send.at[w], p_recv.at[i], w, j)

        @pl.loop(1, wide)
        def _(k):
            wide_peak(k).start()

        def from_wide(k):
            s = (i + k) % wide
            return remote(peak_out, peak_in.at[s], p_send.at[s], p_recv.at[s], s, j)

        peak_mid[...] = peak_out[...]

        @pl.loop(1, wide)
        def _(k):
            from_wide(k).wait_recv()
            peak_mid[...] = jnp.maximum(peak_mid[...], peak_in[(i + k) % wide])

        def narrow_peak(k):
            n = (j + k) % narrow
            return remote(peak_mid, peak_all.at[j], n_send.at[n], n_recv.at[j], i, n)

        def from_narrow(k):
            s = (j + k) % narrow
            return remote(peak_mid, peak_all.at[s], n_send.at[s], n_recv.at[s], i, s)

        @pl.loop(1, narrow)
        def _(k):
            narrow_peak(k).start()


        passed = ((0, -1, slots - 1), (groups - 1, 1, 0))

        def forward(n, s):
            b, near, slot = passed[n]
            return remote(
                arrived.at[s, b + 1, pl.ds(0, deep)], arrived.at[s, slot, pl.ds(0, deep)],
                f_send.at[n, s], f_recv.at[n, s], i, j + near,
            )

        for b in range(groups):
            pltpu.make_async_copy(
                packed.at[b, pl.ds(i * own_z, deep)], arrived.at[i, b + 1, pl.ds(0, deep)], a_sem.at[b]
            ).wait()

            @pl.loop(0, wide)
            def _(k, b=b):
                s = (i + wide - k) % wide

                @pl.when(k > 0)
                def _():
                    remote(
                        packed.at[b, pl.ds(s * own_z, deep)], arrived.at[s, b + 1, pl.ds(0, deep)],
                        a_send.at[b, s], a_recv.at[b, s], s, j,
                    ).wait_recv()

                for n in range(2):
                    if passed[n][0] == b:
                        @pl.when(has[(0, passed[n][1])])
                        def _(n=n):
                            forward(n, s).start()

            unpack(b + 1)

        peak_all[j] = peak_mid[...]

        @pl.loop(1, narrow)
        def _(k):
            from_narrow(k).wait_recv()
            peak_all[j] = jnp.maximum(peak_all[j], peak_all[(j + k) % narrow])

        for n in range(2):
            @pl.when(has[(0, -passed[n][1])])
            def _(n=n):
                @pl.loop(0, wide)
                def _(s):
                    forward(n, s).wait_recv()

            unpack(passed[n][2])

        for n in range(2):
            @pl.when(has[(0, passed[n][1])])
            def _(n=n):
                @pl.loop(0, wide)
                def _(s):
                    forward(n, s).wait_send()

        for b in range(groups):
            @pl.loop(1, wide)
            def _(k, b=b):
                w = (i + k) % wide
                remote(
                    packed.at[b, pl.ds(w * own_z, deep)], arrived.at[i, b + 1, pl.ds(0, deep)],
                    a_send.at[b, w], a_recv.at[b, i], w, j,
                ).wait_send()

        @pl.loop(1, wide)
        def _(k):
            wide_peak(k).wait_send()

        @pl.loop(1, narrow)
        def _(k):
            narrow_peak(k).wait_send()

        for dy in (-1, 1):
            @pl.when(has[(0, dy)])
            def _(dy=dy):
                for l in range(3):
                    y_copy(dy, l).wait_send()
        for dx in (-1, 1):
            @pl.when(has[(dx, 0)])
            def _(dx=dx):
                for l in range(3):
                    for b in range(groups):
                        x_copy(dx, l, b).wait_send()
        for dx, dy in around[4:]:
            @pl.when(has[(dx, dy)])
            def _(dx=dx, dy=dy):
                c_copy(dx, dy).wait_send()
        for k in range(8):
            @pl.when(has[around[k]])
            def _(k=k):
                lev_send_copy(k).wait_send()

    def plane_growth(source, gp, gm, begin, end, done):
        if end <= begin:
            return
        row = lax.broadcasted_iota(jnp.int32, (8, lanes), 0)
        batch = most(end - begin, (6, 4, 3, 2, 1))

        def one_plane(z):
            before, _ = along_rows(source, z, SIDE - 4, 8)
            before = pltpu.roll(before, 5, 0)
            for c in range(groups):
                at = pl.ds(SIDE + 8 * c, 8)
                here, plus = along_rows(source, z, SIDE + 8 * c, 8)
                moved = pltpu.roll(here, 1, 0)
                up_y, down_y = godunov(jnp.where(row == 0, before, moved), plus)
                before = moved
                up_x, down_x = godunov(*along_lanes(source[z, at, :]))
                up = gp[z, at, :] + (up_y + up_x)
                down = gm[z, at, :] + (down_y + down_x)
                if done is None:
                    gp[z, at, :] = jnp.sqrt(up)
                    gm[z, at, :] = jnp.sqrt(down)
                else:
                    done(z, at, c, up, down)

        @pl.loop(0, (end - begin) // batch)
        def _(k):
            for r in range(batch):
                one_plane(begin + batch * k + r)


    def march_phase():
        scale = jnp.max(peak_all[j]) + 1e-06

        @pl.loop(0, deep)
        def _(z):
            for lo in range(0, rows, 16):
                at = pl.ds(lo, 16)
                held = one[z, at, :]
                velocity = jnp.where(inside(z, lo, held.shape), held / scale - 0.5, 0.0)
                one[z, at, :] = velocity
                pull[z, at, :] = pull[z, at, :] * velocity

        top, bottom = MARGIN, MARGIN + own_z
        edge = 6
        source, target = one, two
        lane = lax.broadcasted_iota(jnp.int32, (8, lanes), 1)
        for step in range(EXT_PASSES):
            last = step == EXT_PASSES - 1
            lo, chunks = (SIDE, groups) if last else (SIDE - 4, groups + 1)

            def extend(planes, source=source, target=target, lo=lo, chunks=chunks, last=last):
                spots = [(z, lo + 8 * c) for z in planes for c in range(chunks)]
                mids = [source[z, pl.ds(start, 8), :] for z, start in spots]
                lows = [pltpu.roll(mid, 1, 1) for mid in mids]
                highs = [pltpu.roll(mid, lanes - 1, 1) for mid in mids]
                for (z, start), low, high in zip(spots, lows, highs):
                    at = pl.ds(start, 8)
                    total = source[z - 1, at, :] + source[z + 1, at, :]
                    total = total + (source[z, pl.ds(start - 1, 8), :] + source[z, pl.ds(start + 1, 8), :])
                    low = jnp.where(lane == 0, 0.0, low)
                    high = jnp.where(lane == lanes - 1, 0.0, high)
                    value = pull[z, at, :] + keep[z, at, :] * (total + (low + high))
                    target[z, at, :] = value
                    if last:
                        growth = jnp.where(value > 0.0, gp[z, at, :], gm[z, at, :])
                        psi[z, at, :] = phi[z, at, :] - (TIME_STEP / 6.0) * (value * growth)

            def extend_all(begin, end, extend=extend):
                if end <= begin:
                    return
                size = most(end - begin, (9, 13, 10, 8, 6, 5, 4, 3, 2, 1))

                @pl.loop(0, (end - begin) // size)
                def _(k):
                    extend([begin + size * k + r for r in range(size)])

            if last:
                extend_all(top, top + edge)
                extend_all(bottom - edge, bottom)
                step_do(0, psi, 0, "start")
                extend_all(top + edge, bottom - edge)
                step_do(0, psi, 1, "start")
            else:
                extend_all(step + 1, deep - step - 1)
            source, target = target, source
        speed = source

        source, target = psi, phi
        for step in range(1, HJ_STEPS):
            final = step == HJ_STEPS - 1

            def planes_of(begin, end, c, source=source):
                along_planes(source, gp, gm, begin, end, pl.ds(pl.multiple_of(SIDE + 8 * c, 8), 8))

            planes_of(top + REACH, bottom - REACH, 0)
            for k in (2, 3):
                step_do(step - 1, source, k, "start")

            @pl.loop(1, groups)
            def _(c, planes_of=planes_of):
                planes_of(top + REACH, bottom - REACH, c)

            for k in (0, 1):
                step_do(step - 1, source, k, "wait_recv")

            @pl.loop(0, groups)
            def _(c, planes_of=planes_of):
                planes_of(top, top + REACH, c)
                planes_of(bottom - REACH, bottom, c)

            for k in (2, 3):
                step_do(step - 1, source, k, "wait_recv")

            def done(z, at, c, up, down, source=source, target=target, final=final):
                rate = speed[z, at, :]
                growth = jnp.sqrt(jnp.where(rate > 0.0, up, down))
                value = source[z, at, :] - (TIME_STEP / 6.0) * (rate * growth)
                if final:
                    next_ref[z - MARGIN, pl.ds(8 * c, 8), :] = value
                    speed_ref[z - MARGIN, pl.ds(8 * c, 8), :] = rate
                else:
                    target[z, at, :] = value

            if final:
                plane_growth(source, gp, gm, top, bottom, done)
            else:
                plane_growth(source, gp, gm, top, top + edge, done)
                plane_growth(source, gp, gm, bottom - edge, bottom, done)
                step_do(step, target, 0, "start")
                plane_growth(source, gp, gm, top + edge, bottom - edge, done)
                step_do(step, target, 1, "start")
            for k in range(4):
                step_do(step - 1, source, k, "wait_send")
            source, target = target, source

    pl.run_scoped(
        energy_phase,
        pltpu.VMEM((fields, size_x + 3, tiles, size_y + 16, 128), f32),
        pltpu.VMEM((fields, size_x + 3, tiles, size_y + 16, 128), f32),
    )
    march_phase()


def per_device(displacement, material, level_set, wide, narrow):
    own_z, own_y, lanes = level_set.shape
    loads, comps, size_x, size_y, size_z = displacement.shape
    fields = loads * comps
    deep = own_z + 2 * MARGIN
    groups = own_y // 8
    tiles = size_z // 128
    padded = -(-(size_z + 2 * MARGIN) // 8) * 8
    result = jax.ShapeDtypeStruct((own_z, own_y, lanes), f32)
    dma = pltpu.SemaphoreType.DMA
    vmem = pl.BlockSpec(memory_space=pltpu.VMEM)
    hbm = pl.BlockSpec(memory_space=pl.ANY)
    level, speed = pl.pallas_call(
        functools.partial(kernel, wide=wide, narrow=narrow),
        out_shape=(result, result),
        in_specs=[hbm, vmem, hbm],
        out_specs=(vmem, vmem),
        scratch_shapes=[
            pltpu.VMEM((fields, size_x + 3, size_y + 8, size_z), f32),
            pltpu.VMEM((tiles, size_x * size_y, 128), f32),
            pltpu.VMEM((tiles, size_x * size_y, 128), f32),
            pltpu.VMEM((groups, padded, 128), f32),
            pltpu.VMEM((wide, groups + 2, -(-deep // 8) * 8, 128), f32),
            *[pltpu.VMEM((deep, own_y + 2 * SIDE, lanes), f32)] * 8,
            pltpu.VMEM((8, 128), f32),
            pltpu.VMEM((wide, 8, 128), f32),
            pltpu.VMEM((8, 128), f32),
            pltpu.VMEM((narrow, 8, 128), f32),
            dma((3,)), dma((2, 3, groups)), dma((2, 3, groups)), dma((2, 3)), dma((2, 3)), dma((4,)), dma((4,)),
            dma, dma((8,)), dma((8,)),
            dma((groups,)), dma((groups, wide)), dma((groups, wide)),
            dma((2, wide)), dma((2, wide)),
            dma((wide,)), dma((wide,)), dma((narrow,)), dma((narrow,)),
            dma((HJ_STEPS - 1, 4)), dma((HJ_STEPS - 1, 4)),
        ],
        compiler_params=pltpu.CompilerParams(
            vmem_limit_bytes=62 << 20, collective_id=0, has_side_effects=True
        ),
    )(
        displacement.reshape(fields, size_x, size_y, size_z),
        jnp.swapaxes(material, 1, 2),
        level_set,
    )

    def finish(level_in, speed_in, level_out, speed_out):
        level_out[...] = level_in[...] + 1.0
        speed_out[...] = speed_in[...]

    return pl.pallas_call(
        finish,
        out_shape=(result, result),
        in_specs=[vmem, vmem],
        out_specs=(vmem, vmem),
    )(level, speed)


def solution(mesh):
    return jax.shard_map(
        functools.partial(per_device, wide=mesh.shape["wide"], narrow=mesh.shape["narrow"]),
        mesh=mesh,
        in_specs=(
            P(None, None, "wide", "narrow", None),
            P("wide", "narrow", None),
            P("wide", "narrow", None),
        ),
        out_specs=(P("wide", "narrow", None), P("wide", "narrow", None)),
        check_vma=False,
    )
```
